32 devices in a mesh: grp: 2 (over x), seq: 8 (over z, y), rep: 2 (over core).
Axes of the slice: x: 2, y: 2, z: 4, core: 2. Of those that a mesh axis runs over, the one named last changes fastest.
Arguments:
- queries: bfloat16 [4, 2048, 1024], P(('grp', 'rep'), None, 'seq'), parts along dimension 0, may hold values from -60 to 60
- key_vectors: bfloat16 [4, 2048, 1024], P(('grp', 'rep'), None, 'seq'), parts along dimension 0, may hold values from -8 to 8
- value_vectors: bfloat16 [4, 2048, 1024], P(('grp', 'rep'), None, 'seq'), parts along dimension 0, may hold values from -6 to 6
- context: bfloat16 [4, 2048, 1024], P(('grp', 'rep'), None, 'seq'), parts along dimension 0, may hold values from -6 to 6
- cotangent: bfloat16 [4, 2048, 1024], P(('grp', 'rep'), None, 'seq'), parts along dimension 0, may hold values from -6 to 6
- out_weight: bfloat16 [4096, 2048], P('grp'), parts along dimension 0, may hold values from -0.125 to 0.125
- membership: int32 [4, 1024], P(('grp', 'rep'), 'seq'), parts along dimension 0, may hold values from 0 to 1, as said below
Outputs:
- grad_queries: bfloat16 [4, 2048, 1024], P(('grp', 'rep'), None, 'seq'), parts along dimension 0
- grad_keys: bfloat16 [4, 2048, 1024], P(('grp', 'rep'), None, 'seq'), parts along dimension 0
- grad_values: bfloat16 [4, 2048, 1024], P(('grp', 'rep'), None, 'seq'), parts along dimension 0
- grad_weight: float32 [4096, 2048], P(('grp', 'seq', 'rep')), parts along dimension 0
The draws below stay inside these ranges and needn't reach their ends.
There are 2 independent parts, one for each index of `grp`. The reference program is written for one: setup_inputs(seed, part) draws one part's arguments, and reference() takes and returns one part's arrays. A program takes and returns all parts, laid end to end along the dimension named above; each array names one. Nothing has to cross between parts.
Inputs may be any that keep to these rules, and one draw needn't show every extreme that they name: Every window has at least one cell with membership 1.
All inputs are finite; a program needn't handle non-finite values.
Results may differ from the reference program's by a relative error of at most 0.0058.
Values may be sent and summed in bfloat16 or wider, within the bound.
A program may use at most 128 MiB of HBM per device.

```python
import math
import jax
import jax.numpy as jnp
from jax import lax

HEADS = 32
DH = 64
D = 2048
WINDOW_CELLS = 1024
WINDOW_REPLICAS = 2


def draw_pair(key):
    random_root_key = jax.random.fold_in(key, 91)
    random_query_draw, random_key_draw, random_query_scale, random_key_scale = jax.random.split(random_root_key, 4)
    shape = (WINDOW_REPLICAS, D, WINDOW_CELLS)
    query_base = jax.random.truncated_normal(random_query_draw, -4.0, 4.0, shape, jnp.float32)
    key_base = jax.random.truncated_normal(random_key_draw, -4.0, 4.0, shape, jnp.float32)
    query_scale = jnp.exp(jax.random.uniform(random_query_scale, (WINDOW_REPLICAS, 1, WINDOW_CELLS), jnp.float32, math.log(0.5), math.log(2.0)))
    random_scale_draw = jnp.exp(jax.random.uniform(random_key_scale, (WINDOW_REPLICAS, 1, WINDOW_CELLS), jnp.float32, math.log(0.5), math.log(2.0)))
    key_out = key_base * random_scale_draw
    query_out = query_base * query_scale
    return (query_out, key_out)


def draw_queries(key, part):
    return draw_pair(key)[0].astype(jnp.bfloat16)


def draw_key_vectors(key, part):
    return draw_pair(key)[1].astype(jnp.bfloat16)


def draw_membership(key, part):
    random_root_key = jax.random.fold_in(key, 53)
    key_coin, key_chosen = jax.random.split(random_root_key, 2)
    coin_flip = jax.random.randint(key_coin, (WINDOW_REPLICAS, WINDOW_CELLS), 0, 8)
    chosen = jax.random.randint(key_chosen, (WINDOW_REPLICAS, 1), 0, WINDOW_CELLS)
    cell_ids = jnp.arange(WINDOW_CELLS, dtype=jnp.int32)
    return jnp.where((coin_flip > 0) | (cell_ids[None, :] == chosen), 1, 0).astype(jnp.int32)


def raised(drawn, own_key, source, target, blocks, factor):
    def block_of(position):
        return (jnp.arange(drawn.shape[position]) // (drawn.shape[position] // blocks)).reshape((-1,) + (1,) * (drawn.ndim - 1 - position))

    first = jax.random.permutation(own_key, blocks)[block_of(target)]
    second = (block_of(target) + blocks // 2) % blocks
    return jnp.where((block_of(source) == first) | (block_of(source) == second), factor * drawn, drawn)


def steps_of(key, extent, pieces, smallest, high):
    def one(dim, shards_of):
        draws = jax.random.uniform(jax.random.fold_in(jax.random.fold_in(key, 6), dim), (shards_of,), jnp.float32, smallest / len(pieces), high / len(pieces))
        return jnp.repeat(jnp.exp(draws), extent[dim] // shards_of).reshape((-1,) + (1,) * (len(extent) - dim - 1))

    factor_of = one(*pieces[0])
    for cut in pieces[1:]:
        factor_of = factor_of * one(*cut)
    return factor_of


def centred(own_key, extent, spread, reach, pieces=(), kind=jnp.bfloat16):
    drawn = jax.random.normal(own_key, extent, jnp.float32) * spread
    if len(pieces) > 0:
        drawn = steps_of(own_key, extent, pieces, -0.22, 0.18) * drawn
    return jnp.clip(drawn, min=-reach, max=reach).astype(kind)


def gaussian_with(own_key, shape, deviation, reach, cuts, heavy, kind=jnp.bfloat16):
    values = deviation * jax.random.normal(own_key, shape, jnp.float32)
    if cuts:
        values = values * steps_of(own_key, shape, cuts, -0.22, 0.18)
    return jnp.clip(raised(values, jax.random.fold_in(own_key, 3), *heavy), -reach, reach).astype(kind)


def setup_inputs(seed: int = 0, part: int = 0) -> dict:
    keys = jax.random.split(jax.random.key(seed), 8)
    own_keys = jax.random.split(jax.random.fold_in(keys[7], part), 8)
    queries = draw_queries(jax.random.fold_in(jax.random.fold_in(keys[7], part), 71), part)
    key_vectors = draw_key_vectors(jax.random.fold_in(jax.random.fold_in(keys[7], part), 71), part)
    value_vectors = centred(own_keys[2], (WINDOW_REPLICAS, D, WINDOW_CELLS), 1.0, 6.0, ((0, 2), (2, 8)))
    context = gaussian_with(own_keys[3], (WINDOW_REPLICAS, D, WINDOW_CELLS), 1.0, 6.0, ((0, 2), (2, 8)), (2, 1, 8, 2.0))
    cotangent = centred(own_keys[4], (WINDOW_REPLICAS, D, WINDOW_CELLS), 1.0, 6.0, ((0, 2), (2, 8)))
    out_weight = centred(own_keys[5], (D, D), D ** -0.5, 0.125)
    membership = draw_membership(jax.random.fold_in(jax.random.fold_in(keys[7], part), 71), part)
    return {"queries": queries, "key_vectors": key_vectors, "value_vectors": value_vectors, "context": context, "cotangent": cotangent, "out_weight": out_weight, "membership": membership}


def head_grads(query_head, key_head, value_head, grad_head, context_head, member_keys):
    score_scale = 1.0 / math.sqrt(DH)
    scores = jnp.dot(query_head.T, key_head, preferred_element_type=jnp.float32) * score_scale
    scores = jnp.where(member_keys[None, :], scores, -jnp.inf)
    highest = lax.optimization_barrier(jnp.max(scores, axis=1, keepdims=True))
    exp_scores = jnp.exp(scores - highest)
    probabilities = exp_scores / lax.optimization_barrier(jnp.sum(exp_scores, axis=1, keepdims=True))
    row_delta = lax.optimization_barrier(jnp.sum(grad_head.astype(jnp.float32) * context_head.astype(jnp.float32), axis=0))
    probs_low = probabilities.astype(jnp.bfloat16)
    grad_value = jnp.dot(grad_head, probs_low, preferred_element_type=jnp.float32).astype(jnp.bfloat16)
    grad_probs = jnp.dot(grad_head.T, value_head, preferred_element_type=jnp.float32)
    grad_scores = (probabilities * (grad_probs - row_delta[:, None]) * score_scale).astype(jnp.bfloat16)
    grad_query = jnp.dot(key_head, grad_scores.T, preferred_element_type=jnp.float32).astype(jnp.bfloat16)
    grad_key = jnp.dot(query_head, grad_scores, preferred_element_type=jnp.float32).astype(jnp.bfloat16)
    return (grad_query, grad_key, grad_value)

def reference(queries, key_vectors, value_vectors, context, cotangent, out_weight, membership):
    grad_context = jnp.stack([jnp.dot(out_weight, cotangent[replica], preferred_element_type=jnp.float32).astype(jnp.bfloat16) for replica in range(WINDOW_REPLICAS)])
    zero_index = jnp.zeros((), jnp.int32)

    def one_pair(pair_index):
        replica = (pair_index // HEADS).astype(jnp.int32)
        head_index = (pair_index % HEADS).astype(jnp.int32)
        first_row = (head_index * DH).astype(jnp.int32)

        def select(array):
            return lax.dynamic_slice(array, (replica, first_row, zero_index), (1, DH, WINDOW_CELLS))[0]
        member_keys = lax.dynamic_index_in_dim(membership, replica, 0, keepdims=False) > 0
        return head_grads(select(queries), select(key_vectors), select(value_vectors), select(grad_context), select(context), member_keys)
    results = lax.map(one_pair, jnp.arange(WINDOW_REPLICAS * HEADS, dtype=jnp.int32))
    grad_queries = results[0].reshape(WINDOW_REPLICAS, D, WINDOW_CELLS)
    grad_keys = results[1].reshape(WINDOW_REPLICAS, D, WINDOW_CELLS)
    grad_values = results[2].reshape(WINDOW_REPLICAS, D, WINDOW_CELLS)
    grad_weight = jnp.zeros((D, D), jnp.float32)
    for replica in range(WINDOW_REPLICAS):
        grad_weight = grad_weight + jnp.dot(context[replica], cotangent[replica].T, preferred_element_type=jnp.float32)
    return (grad_queries, grad_keys, grad_values, grad_weight)
```

```python
import functools
import math

import jax
import jax.numpy as jnp
from jax import lax
from jax.experimental import pallas as pl
from jax.experimental.pallas import tpu as pltpu
from jax.sharding import PartitionSpec as P

DH = 64
MESH = pl.DeviceIdType.MESH
CHUNKS = 4


def kernel(n, ny, *refs):
    (q_ref, k_ref, v_ref, c_ref, cot_ref, w_ref, m_ref,
     dq_out, dk_out, dv_out, gw_out,
     q_buf, k_buf, v_buf, c_buf, g_buf, dq_buf, dk_buf, dv_buf,
     cot, w_buf, m_buf, gw, gw_in, k_acc, v_acc,
     w_sem, own_sem, m_send, m_recv, in_send, in_recv,
     ag_send, ag_recv, out_send, out_recv, gw_send, gw_recv, gw_sem) = refs
    me = lax.axis_index("seq")
    rep = lax.axis_index("rep")
    nz = n // ny
    z, y = me // ny, me % ny
    rows, length = q_buf.shape
    cells = length // n
    features = cot.shape[0]
    heads = rows // DH
    half = rows // 2
    piece = features // CHUNKS
    inputs = ((k_ref, k_buf), (q_ref, q_buf), (v_ref, v_buf), (c_ref, c_buf))
    outputs = ((dv_buf, dv_out), (dq_buf, dq_out), (dk_buf, dk_out))

    def cols(seq):
        return pl.ds(pl.multiple_of(seq * cells, cells), cells)

    def head_rows(h, owner=0):
        return pl.ds(pl.multiple_of(owner * rows + h * DH, DH), DH)

    barrier = pltpu.get_barrier_semaphore()
    for k in range(1, n):
        pl.semaphore_signal(barrier, inc=1, device_id={"seq": (me + k) % n}, device_id_type=MESH)
    pl.semaphore_signal(barrier, inc=1, device_id={"rep": 1 - rep}, device_id_type=MESH)

    w_copy = pltpu.make_async_copy(
        w_ref.at[pl.ds(pl.multiple_of(me * rows, rows), rows), :], w_buf, w_sem
    )
    w_copy.start()
    own_copy = pltpu.make_async_copy(cot_ref.at[0], cot.at[:, cols(me)], own_sem)
    own_copy.start()
    pltpu.make_async_copy(m_ref, m_buf.at[:, cols(me)], m_recv).start()

    pl.semaphore_wait(barrier, n)

    def ag_copy(step, part, origin, way, target):
        part_rows = pl.ds(part * piece, piece)
        landing = cot.at[part_rows, cols(origin)]
        source = cot_ref.at[0, part_rows, :] if step == 0 else landing
        return pltpu.make_async_remote_copy(
            src_ref=source,
            dst_ref=landing,
            send_sem=ag_send.at[way, step, part],
            recv_sem=ag_recv.at[part, origin],
            device_id={"seq": target},
            device_id_type=MESH,
        )

    def ag_wait(part, origin):
        landing = cot.at[pl.ds(part * piece, piece), cols(origin)]
        pltpu.make_async_copy(landing, landing, ag_recv.at[part, origin]).wait()

    def ag_step(step, arrived, send):
        for part in range(CHUNKS):
            up, down = z - step, z + step

            def act(origin, way, target):
                copy = ag_copy(step, part, origin, way, target)
                if send:
                    copy.start()
                else:
                    copy.wait_send()

            def cross(origin, way):
                if ny == 2:
                    act(origin, way, z * ny + 1 - y)

            @pl.when(up >= 0)
            def _():
                if arrived:
                    ag_wait(part, up * ny + y)

                @pl.when(z + 1 < nz)
                def _():
                    act(up * ny + y, 0, me + ny)

                cross(up * ny + y, 2)

            @pl.when(down < nz)
            def _():
                if arrived:
                    ag_wait(part, down * ny + y)

                @pl.when(z >= 1)
                def _():
                    act(down * ny + y, 1, me - ny)

                if step > 0:
                    cross(down * ny + y, 3)

    def keep_inputs(h, carry):
        for t, (ref, buf) in enumerate(inputs):
            pltpu.make_async_copy(
                ref.at[0, head_rows(h, me), :], buf.at[head_rows(h), cols(me)], in_recv.at[t, h]
            ).start()
        return carry

    def send_inputs(h, column, first):
        def to_peer(k, carry):
            peer = (z + k) % nz * ny + column
            for t, (ref, buf) in enumerate(inputs):
                pltpu.make_async_remote_copy(
                    src_ref=ref.at[0, head_rows(h, peer), :],
                    dst_ref=buf.at[head_rows(h), cols(me)],
                    send_sem=in_send.at[t],
                    recv_sem=in_recv.at[t, h],
                    device_id={"seq": peer},
                    device_id_type=MESH,
                ).start()
            return carry

        lax.fori_loop(first, nz, to_peer, 0)

    def send_members(k, carry):
        pltpu.make_async_remote_copy(
            src_ref=m_ref,
            dst_ref=m_buf.at[:, cols(me)],
            send_sem=m_send,
            recv_sem=m_recv,
            device_id={"seq": (me + k) % n},
            device_id_type=MESH,
        ).start()
        return carry

    sent = 0
    for step in range(nz):
        ag_step(step, arrived=step > 0, send=True)
        if step == 0:
            lax.fori_loop(1, n, send_members, 0)
            lax.fori_loop(0, heads, keep_inputs, 0)
        upto = -(-step * heads // nz)
        for h in range(sent, upto):
            for column, first in ((y, 1), (1 - y, 0))[:ny]:
                send_inputs(h, column, first)
        sent = upto
    for h in range(sent, heads):
        for column, first in ((y, 1), (1 - y, 0))[:ny]:
            send_inputs(h, column, first)
    if ny == 2:
        for origin_z in range(nz):
            for part in range(CHUNKS):
                ag_wait(part, origin_z * ny + 1 - y)
    own_copy.wait()
    w_copy.wait()

    block = min(256, length)

    def project(i, carry):
        at = pl.ds(pl.multiple_of(i * block, block), block)
        g_buf[:, at] = jnp.dot(
            w_buf[...], cot[:, at], preferred_element_type=jnp.float32
        ).astype(jnp.bfloat16)
        return carry

    lax.fori_loop(0, length // block, project, 0)
    pltpu.make_async_copy(m_buf, m_buf, m_recv).wait()

    scale = 1.0 / math.sqrt(DH)
    tile = 256 if length <= 2048 else 128

    def one_head(h, carry):
        mine = head_rows(h)
        for t, (_, buf) in enumerate(inputs):
            pltpu.make_async_copy(buf.at[mine], buf.at[mine], in_recv.at[t, h]).wait()
        member = m_buf[...] > 0
        keys = k_buf[mine, :]
        values = v_buf[mine, :]
        keys_scaled = keys * jnp.bfloat16(scale)
        k_acc[...] = jnp.zeros_like(k_acc)
        v_acc[...] = jnp.zeros_like(v_acc)

        def one_tile(i, inner):
            at = pl.ds(pl.multiple_of(i * tile, tile), tile)
            query = q_buf[mine, at] * jnp.bfloat16(scale)
            grad = g_buf[mine, at]
            products = grad.astype(jnp.float32) * c_buf[mine, at].astype(jnp.float32)
            delta = jnp.sum(products.T, axis=1, keepdims=True)
            first = (((0,), (0,)), ((), ()))
            scores = lax.dot_general(query, keys, first, preferred_element_type=jnp.float32)
            scores = jnp.where(member, scores, -jnp.inf)
            exps = jnp.exp(scores - jnp.max(scores, axis=1, keepdims=True))
            probs = exps * (1.0 / jnp.sum(exps, axis=1, keepdims=True))
            v_acc[...] += jnp.dot(
                grad, probs.astype(jnp.bfloat16), preferred_element_type=jnp.float32
            )
            grad_probs = lax.dot_general(grad, values, first, preferred_element_type=jnp.float32)
            grad_scores = (probs * (grad_probs - delta)).astype(jnp.bfloat16)
            dq_buf[mine, at] = lax.dot_general(
                keys_scaled, grad_scores, (((1,), (1,)), ((), ())),
                preferred_element_type=jnp.float32,
            ).astype(jnp.bfloat16)
            k_acc[...] += jnp.dot(query, grad_scores, preferred_element_type=jnp.float32)
            return inner

        lax.fori_loop(0, length // tile, one_tile, 0)
        dk_buf[mine, :] = k_acc[...].astype(jnp.bfloat16)
        dv_buf[mine, :] = v_acc[...].astype(jnp.bfloat16)
        for t, (buf, out) in enumerate(outputs):
            pltpu.make_async_copy(
                buf.at[mine, cols(me)], out.at[0, head_rows(h, me), :], out_recv.at[t]
            ).start()

        def to_peer(k, inner):
            peer = (me + k) % n
            for t, (buf, out) in enumerate(outputs):
                pltpu.make_async_remote_copy(
                    src_ref=buf.at[mine, cols(peer)],
                    dst_ref=out.at[0, head_rows(h, me), :],
                    send_sem=out_send.at[t],
                    recv_sem=out_recv.at[t],
                    device_id={"seq": peer},
                    device_id_type=MESH,
                ).start()
            return inner

        lax.fori_loop(1, n, to_peer, 0)
        return carry

    lax.fori_loop(0, heads, one_head, 0)

    width = min(256, features)

    def weight_part(i, carry):
        at = pl.ds(pl.multiple_of(i * width, width), width)
        gw[:, at] = lax.dot_general(
            c_buf[...], cot[at, :], (((1,), (1,)), ((), ())), preferred_element_type=jnp.float32
        )
        return carry

    lax.fori_loop(0, features // width, weight_part, 0)
    swap = pltpu.make_async_remote_copy(
        src_ref=gw.at[pl.ds(pl.multiple_of((1 - rep) * half, half), half), :],
        dst_ref=gw_in,
        send_sem=gw_send,
        recv_sem=gw_recv,
        device_id={"rep": 1 - rep},
        device_id_type=MESH,
    )
    swap.start()
    swap.wait()
    gw_in[...] += gw[pl.ds(pl.multiple_of(rep * half, half), half), :]
    total = pltpu.make_async_copy(gw_in, gw_out, gw_sem)
    total.start()

    for step in range(nz):
        ag_step(step, arrived=False, send=False)
    others = (n - 1) * rows
    for t, (ref, _) in enumerate(inputs):
        gone = ref.at[0, pl.ds(0, others), :]
        pltpu.make_async_copy(gone, gone, in_send.at[t]).wait()
    gone = m_buf.at[:, pl.ds(0, (n - 1) * cells)]
    pltpu.make_async_copy(gone, gone, m_send).wait()
    for t, (buf, out) in enumerate(outputs):
        gone = buf.at[:, pl.ds(0, (n - 1) * cells)]
        pltpu.make_async_copy(gone, gone, out_send.at[t]).wait()
        pltpu.make_async_copy(out, out, out_recv.at[t]).wait()
    total.wait()


def paired(*refs):
    (q_ref, k_ref, v_ref, c_ref, cot_ref, w_ref, m_ref,
     dq_out, dk_out, dv_out, gw_out,
     q_buf, k_buf, v_buf, g_buf, exps, w_buf, cot, ctx, ctx_own, g_col,
     dq_buf, dk_buf, dv_buf, dq_in, dq_sum,
     part, part_in, y_out, y_in, far_out, far_in, gw_sum,
     m_buf, bias, tops, lse, lse_in, delta_out, delta, k_turn, v_turn, k_acc, v_acc,
     w_sem, own_sem, m_send, m_recv, q_send, q_recv, k_send, k_recv, v_send, v_recv,
     cot_send, cot_recv, ctx_send, ctx_recv, delta_send, delta_recv, g_send, g_recv,
     lse_send, lse_recv, dq_send, dq_recv, dk_send, dk_recv, dv_send, dv_recv,
     rep_send, rep_recv, y_send, y_recv, far_send, far_recv, res_sem) = refs
    me = lax.axis_index("seq")
    rep = lax.axis_index("rep")
    z, y = me // 2, me % 2
    half = z // 2
    near = 2 * half + 1 - z % 2
    mirror = 3 - z
    outer = jnp.logical_or(z == 0, z == 3)
    inner = jnp.logical_not(outer)
    features, cells = cot_ref.shape[1], cot_ref.shape[2]
    rows = features // 8
    heads = rows // DH
    length = 8 * cells
    low = jnp.bfloat16
    scale = 1.0 / math.sqrt(DH)

    def span(start, size):
        return pl.ds(pl.multiple_of(start * size, size), size)

    def group(zt, yt, j):
        first = jnp.minimum(zt, 3 - zt)
        return 2 * (first if j == 0 else 3 - first) + yt

    def slot(j):
        return pl.ds(j * rows, rows)

    def qcols(zt, yt):
        return span(yt * 4 + zt, cells)

    def kcols(zt, yt):
        return span(zt % 2 * 2 + yt, cells)

    def remote(src, dst, send, recv, zt, yt):
        pltpu.make_async_remote_copy(
            src_ref=src, dst_ref=dst, send_sem=send, recv_sem=recv,
            device_id={"seq": zt * 2 + yt}, device_id_type=MESH,
        ).start()

    def to_rep(src, dst, send, recv):
        pltpu.make_async_remote_copy(
            src_ref=src, dst_ref=dst, send_sem=send, recv_sem=recv,
            device_id={"rep": 1 - rep}, device_id_type=MESH,
        ).start()

    def local(src, dst, sem):
        pltpu.make_async_copy(src, dst, sem).start()

    def done(ref, sem):
        pltpu.make_async_copy(ref, ref, sem).wait()

    barrier = pltpu.get_barrier_semaphore()
    for k in range(1, 8):
        pl.semaphore_signal(barrier, inc=1, device_id={"seq": (me + k) % 8}, device_id_type=MESH)
    pl.semaphore_signal(barrier, inc=1, device_id={"rep": 1 - rep}, device_id_type=MESH)

    local(cot_ref.at[0], cot.at[:, span(z, cells)], own_sem.at[0])
    for i in range(4):
        strip = pl.ds(i * features // 4, features // 4)
        local(w_ref.at[strip, :], w_buf.at[strip, :], w_sem.at[i])
    local(c_ref.at[0], ctx_own, own_sem.at[1])
    local(m_ref, m_buf.at[:, kcols(z, y)], m_recv)
    for j in range(2):
        mine = span(group(z, y, j), rows)
        local(k_ref.at[0, mine, :], k_buf.at[slot(j), kcols(z, y)], k_recv.at[j])
        local(q_ref.at[0, mine, :], q_buf.at[slot(j), qcols(z, y)], q_recv.at[j])
        local(v_ref.at[0, mine, :], v_buf.at[slot(j), kcols(z, y)], v_recv.at[j])

    pl.semaphore_wait(barrier, 8)

    def send_q(zt, yt, j):
        remote(q_ref.at[0, span(group(zt, yt, j), rows), :], q_buf.at[slot(j), qcols(z, y)],
               q_send, q_recv.at[j], zt, yt)

    def send_k(zt, yt, j):
        remote(k_ref.at[0, span(group(zt, yt, j), rows), :], k_buf.at[slot(j), kcols(z, y)],
               k_send, k_recv.at[j], zt, yt)

    def send_v(zt, yt, j):
        remote(v_ref.at[0, span(group(zt, yt, j), rows), :], v_buf.at[slot(j), kcols(z, y)],
               v_send, v_recv.at[j], zt, yt)

    def send_ctx(zt):
        remote(c_ref.at[0, span(zt // 2, 4 * rows), :], ctx.at[:, span(z, cells)],
               ctx_send, ctx_recv, zt, y)

    piece = features // CHUNKS

    def send_cot(zt):
        for i in range(CHUNKS):
            strip = pl.ds(i * piece, piece)
            remote(cot_ref.at[0, strip, :], cot.at[strip, span(z, cells)],
                   cot_send, cot_recv.at[z, i], zt, y)

    def send_m():
        for zt, yt in ((near, y), (near, 1 - y), (z, 1 - y)):
            remote(m_ref, m_buf.at[:, kcols(z, y)], m_send, m_recv, zt, yt)

    both = (y, 1 - y)

    @pl.when(outer)
    def _():
        send_cot(near)
        for j in range(2):
            for yt in both:
                send_q(mirror, yt, j)
            send_k(z, 1 - y, j)
            send_q(z, 1 - y, j)
            if j == 0:
                send_ctx(near)
                send_ctx(3 - near)
                send_m()
            for yt in both:
                send_k(near, yt, j)
            for yt in both:
                send_q(near, yt, j)
            for yt in both:
                send_q(3 - near, yt, j)
            send_v(z, 1 - y, j)
            for yt in both:
                send_v(near, yt, j)

    @pl.when(inner)
    def _():
        send_cot(mirror)
        local(c_ref.at[0, span(half, 4 * rows), :], ctx.at[:, span(z, cells)], ctx_recv)
        for yt in both:
            send_k(near, yt, 0)
        for yt in both:
            send_q(near, yt, 0)
        send_k(z, 1 - y, 0)
        send_q(z, 1 - y, 0)

    def project(zt, first, count):
        for i in range(first, first + count):
            strip = pl.ds(i * features // 4, features // 4)
            g_col[strip, span(zt, cells)] = jnp.dot(
                w_buf[strip, :], cot[:, span(zt, cells)], preferred_element_type=jnp.float32
            ).astype(low)

    def project_middle(zt):
        strip = pl.ds(features // 4, features // 2)
        g_col[strip, span(zt, cells)] = jnp.dot(
            w_buf[strip, :], cot[:, span(zt, cells)], preferred_element_type=jnp.float32
        ).astype(low)

    def hand_g(zt, own, far):
        for j in range(2):
            if far:
                for yt in both:
                    remote(g_col.at[span(group(near, yt, j), rows), span(zt, cells)],
                           g_buf.at[slot(j), qcols(zt, y)], g_send, g_recv.at[j], near, yt)
            if own:
                remote(g_col.at[span(group(z, 1 - y, j), rows), span(zt, cells)],
                       g_buf.at[slot(j), qcols(zt, y)], g_send, g_recv.at[j], z, 1 - y)
        for j in range(2):
            g_buf[slot(j), qcols(zt, y)] = g_col[span(group(z, y, j), rows), span(zt, cells)]

    done(cot_ref.at[0], own_sem.at[0])
    for i in range(4):
        strip = pl.ds(i * features // 4, features // 4)
        done(w_buf.at[strip, :], w_sem.at[i])
        project(z, i, 1)

    @pl.when(outer)
    def _():
        hand_g(z, True, False)

    @pl.when(inner)
    def _():
        hand_g(z, True, True)

    done(ctx_own, own_sem.at[1])
    for zp in range(2):
        for yt in range(2):
            for j in range(2):
                g = 2 * (zp if j == 0 else 3 - zp) + yt
                at = pl.ds(g * rows, rows)
                products = g_col[at, span(z, cells)].astype(jnp.float32) * ctx_own[at, :].astype(jnp.float32)
                delta_out[2 * zp + yt, pl.ds(j * heads, heads), :] = jnp.sum(
                    products.reshape(heads, DH, cells), axis=1
                )

    def kind(zt, yt):
        return 2 * jnp.minimum(zt, 3 - zt) + yt

    local(delta_out.at[kind(z, y)], delta.at[:, qcols(z, y)], delta_recv)
    for k in range(1, 8):
        peer = (me + k) % 8
        remote(delta_out.at[kind(peer // 2, peer % 2)], delta.at[:, qcols(z, y)],
               delta_send, delta_recv, peer // 2, peer % 2)

    def cot_done(zt, i):
        done(cot.at[pl.ds(i * piece, piece), span(zt, cells)], cot_recv.at[zt, i])

    @pl.when(inner)
    def _():
        for i in range(CHUNKS):
            strip = pl.ds(i * piece, piece)
            cot_done(near, i)
            landed = cot.at[strip, span(near, cells)]
            remote(landed, landed, cot_send, cot_recv.at[near, i], mirror, y)
        send_m()
        for yt in both:
            send_q(3 - near, yt, 0)
        send_ctx(mirror)
        for yt in both:
            send_q(mirror, yt, 0)
        for yt in both:
            send_v(near, yt, 0)
        send_v(z, 1 - y, 0)
        for yt in both:
            send_k(near, yt, 1)
            send_q(near, yt, 1)
        send_k(z, 1 - y, 1)
        send_q(z, 1 - y, 1)
        for yt in both:
            send_q(3 - near, yt, 1)
        for yt in both:
            send_q(mirror, yt, 1)
        for yt in both:
            send_v(near, yt, 1)
        send_v(z, 1 - y, 1)
        project_middle(near)
        hand_g(near, True, False)
        for i in range(CHUNKS):
            cot_done(mirror, i)
        project(mirror, 0, 4)
        hand_g(mirror, True, True)

    done(m_buf, m_recv)
    shut = jnp.where(m_buf[...] > 0, 0.0, -1e30).astype(jnp.float32)
    bias[...] = jnp.broadcast_to(shut, (cells, length // 2)).T

    tile = 2 * cells
    tiles = length // tile
    first = (((0,), (0,)), ((), ()))
    last = (((1,), (1,)), ((), ()))

    def score_head(h, carry):
        mine = span(h, DH)
        k_turn[...] = (k_buf[mine, :] * low(scale)).T

        def one_tile(i, inner_carry):
            at = span(i, tile)
            scores = jnp.dot(k_turn[...], q_buf[mine, at], preferred_element_type=jnp.float32)
            scores = scores + jnp.concatenate([bias[...], bias[...]], axis=1)
            top = jnp.max(scores, axis=0, keepdims=True)
            grown = jnp.exp(scores - top)
            exps[h, :, at] = grown
            tops[h, :, at] = top
            lse[h, :, at] = top + jnp.log(jnp.sum(grown, axis=0, keepdims=True))
            return inner_carry

        lax.fori_loop(0, tiles, one_tile, 0)
        return carry

    def score(j):
        done(k_buf.at[slot(j), :], k_recv.at[j])
        done(q_buf.at[slot(j), :], q_recv.at[j])
        lax.fori_loop(j * heads, (j + 1) * heads, score_head, 0)
        some = pl.ds(j * heads, heads)
        remote(lse.at[some], lse_in.at[some], lse_send, lse_recv.at[j], mirror, y)

    def grad_head(j, h, carry):
        mine = span(h, DH)
        keys = k_buf[mine, :] * low(scale)
        v_turn[...] = v_buf[mine, :].T
        k_acc[...] = jnp.zeros_like(k_acc)
        v_acc[...] = jnp.zeros_like(v_acc)

        def one_tile(i, inner_carry):
            at = span(i, tile)
            ours, theirs = lse[h, :, at], lse_in[h, :, at]
            high = jnp.maximum(ours, theirs)
            total = high + jnp.log(jnp.exp(ours - high) + jnp.exp(theirs - high))
            probs = exps[h, :, at] * jnp.exp(tops[h, :, at] - total)
            grad = g_buf[mine, at]
            v_acc[...] += lax.dot_general(
                grad, probs.astype(low), last, preferred_element_type=jnp.float32
            )
            grad_probs = jnp.dot(v_turn[...], grad, preferred_element_type=jnp.float32)
            grad_scores = (probs * (grad_probs - delta[pl.ds(h, 1), at])).astype(low)
            dq_buf[mine, at] = jnp.dot(
                keys, grad_scores, preferred_element_type=jnp.float32
            ).astype(low)
            query = q_buf[mine, at] * low(scale)
            k_acc[...] += lax.dot_general(
                query, grad_scores, last, preferred_element_type=jnp.float32
            )
            return inner_carry

        lax.fori_loop(0, tiles, one_tile, 0)
        dk_buf[mine, :] = k_acc[...].astype(low)
        dv_buf[mine, :] = v_acc[...].astype(low)
        home = span(group(z, y, j) * heads + h - j * heads, DH)
        pairs = ((dk_buf, dk_out, dk_send, dk_recv), (dv_buf, dv_out, dv_send, dv_recv))
        for buf, out, send, recv in pairs:
            for zt, yt in ((near, y), (near, 1 - y), (z, 1 - y)):
                remote(buf.at[mine, kcols(zt, yt)], out.at[0, home, :], send, recv, zt, yt)
            local(buf.at[mine, kcols(z, y)], out.at[0, home, :], recv)
        for zt in (near, 3 - near, mirror):
            for yt in both:
                remote(dq_buf.at[mine, qcols(zt, yt)], dq_in.at[half, home, :],
                       dq_send, dq_recv, zt, yt)
        remote(dq_buf.at[mine, qcols(z, 1 - y)], dq_in.at[half, home, :],
               dq_send, dq_recv, z, 1 - y)
        local(dq_buf.at[mine, qcols(z, y)], dq_in.at[half, home, :], dq_recv)
        return carry

    def grads(j):
        @pl.when(outer)
        def _():
            done(g_buf.at[slot(j), pl.ds(0, 7 * cells)], g_recv.at[j])

        @pl.when(inner)
        def _():
            done(g_buf.at[slot(j), pl.ds(0, 4 * cells)], g_recv.at[j])

        done(v_buf.at[slot(j), :], v_recv.at[j])
        done(lse_in.at[pl.ds(j * heads, heads)], lse_recv.at[j])
        if j == 0:
            done(delta, delta_recv)
        lax.fori_loop(j * heads, (j + 1) * heads, functools.partial(grad_head, j), 0)

    width = features // CHUNKS
    strip_rows = rows // 2

    def weight_products():
        done(ctx, ctx_recv)
        for i in range(CHUNKS):
            for sub in range(2):
                at = pl.ds(i * width + sub * width // 2, width // 2)
                product = lax.dot_general(ctx[...], cot[at, :], last, preferred_element_type=jnp.float32)
                for g in range(4):
                    for r in range(2):
                        start = (2 * g + r) * strip_rows
                        part[r, pl.ds(g * strip_rows, strip_rows), at] = product[start:start + strip_rows]
            at = pl.ds(i * width, width)
            to_rep(part.at[1 - rep, :, at], part_in.at[:, at], rep_send, rep_recv.at[i])

    def weight_across():
        for i in range(CHUNKS):
            at = pl.ds(i * width, width)
            done(part_in.at[:, at], rep_recv.at[i])
            for zl in range(2):
                theirs = span(2 * zl + 1 - y, strip_rows)
                y_out[pl.ds(zl * strip_rows, strip_rows), at] = (
                    part[rep, theirs, at] + part_in[theirs, at]
                ).astype(low)
            remote(y_out.at[:, at], y_in.at[:, at], y_send, y_recv.at[i], z, 1 - y)

    def weight_finish():
        for i in range(CHUNKS):
            at = pl.ds(i * width, width)
            done(y_in.at[:, at], y_recv.at[i])

            def total(zl):
                ours = span(2 * zl + y, strip_rows)
                return part[rep, ours, at] + part_in[ours, at] + y_in[span(zl, strip_rows), at].astype(jnp.float32)

            far_out[:, at] = total(near % 2).astype(low)
            remote(far_out.at[:, at], far_in.at[:, at], far_send, far_recv.at[i], near, y)
            gw_sum[:, at] = total(z % 2)
        local(gw_sum, gw_out, res_sem.at[1])

    score(0)

    @pl.when(inner)
    def _():
        for i in range(CHUNKS):
            cot_done(3 - near, i)
        project(3 - near, 0, 4)
        hand_g(3 - near, True, True)
        weight_products()

    score(1)

    @pl.when(inner)
    def _():
        weight_across()

    grads(0)

    @pl.when(inner)
    def _():
        weight_finish()

    grads(1)

    @pl.when(outer)
    def _():
        for i in range(CHUNKS):
            at = pl.ds(i * width, width)
            done(far_in.at[:, at], far_recv.at[i])
            gw_sum[:, at] = far_in[:, at].astype(jnp.float32)
        local(gw_sum, gw_out, res_sem.at[1])

    done(dq_in, dq_recv)
    dq_sum[...] = (dq_in[0].astype(jnp.float32) + dq_in[1].astype(jnp.float32)).astype(low)
    local(dq_sum, dq_out.at[0], res_sem.at[0])

    done(q_buf.at[:, pl.ds(0, 7 * cells)], q_send)
    done(k_buf.at[:, pl.ds(0, 3 * cells)], k_send)
    done(v_buf.at[:, pl.ds(0, 3 * cells)], v_send)
    done(m_buf.at[:, pl.ds(0, 3 * cells)], m_send)
    done(delta.at[:, pl.ds(0, 7 * cells)], delta_send)
    done(lse, lse_send)
    done(dq_buf.at[:, pl.ds(0, 7 * cells)], dq_send)
    done(dk_buf.at[:, pl.ds(0, 3 * cells)], dk_send)
    done(dv_buf.at[:, pl.ds(0, 3 * cells)], dv_send)
    done(dk_out, dk_recv)
    done(dv_out, dv_recv)

    @pl.when(outer)
    def _():
        done(cot_ref.at[0], cot_send)
        done(c_ref.at[0], ctx_send)
        done(g_buf.at[:, pl.ds(0, cells)], g_send)

    @pl.when(inner)
    def _():
        done(cot.at[:, pl.ds(0, 2 * cells)], cot_send)
        done(c_ref.at[0, pl.ds(0, 4 * rows), :], ctx_send)
        done(g_buf.at[:, pl.ds(0, 4 * cells)], g_send)
        done(g_buf.at[:, pl.ds(0, 6 * cells)], g_send)
        done(part_in, rep_send)
        done(y_out, y_send)
        done(far_out, far_send)

    done(dq_sum, res_sem.at[0])
    done(gw_sum, res_sem.at[1])


def hand_over(*refs):
    sources, targets, stages, (sem_in, sem_out) = refs[:4], refs[4:8], refs[8:12], refs[12:]
    reads, writes = [], []
    for t in range(4):
        reads.append(pltpu.make_async_copy(sources[t], stages[t], sem_in.at[t]))
        writes.append(pltpu.make_async_copy(stages[t], targets[t], sem_out.at[t]))
    for copy in reads:
        copy.start()
    for read, write in zip(reads, writes):
        read.wait()
        write.start()
    for copy in writes:
        copy.wait()


def paired_call(features, cells, *arrays):
    rows, length = features // 8, 8 * cells
    heads = rows // DH
    low, full = jnp.bfloat16, jnp.float32
    dma = pltpu.SemaphoreType.DMA
    anywhere = pl.BlockSpec(memory_space=pl.ANY)
    vmem = pltpu.VMEM
    part = jax.ShapeDtypeStruct((1, features, cells), low)
    return pl.pallas_call(
        paired,
        out_shape=(part, part, part, jax.ShapeDtypeStruct((rows // 2, features), full)),
        in_specs=[anywhere] * 7,
        out_specs=(anywhere,) * 4,
        scratch_shapes=[
            vmem((2 * rows, length), low),
            vmem((2 * rows, length // 2), low),
            vmem((2 * rows, length // 2), low),
            vmem((2 * rows, length), low),
            vmem((2 * heads, length // 2, length), full),
            vmem((features, features), low),
            vmem((features, 4 * cells), low),
            vmem((4 * rows, 4 * cells), low),
            vmem((features, cells), low),
            vmem((features, 4 * cells), low),
            vmem((2 * rows, length), low),
            vmem((2 * rows, length // 2), low),
            vmem((2 * rows, length // 2), low),
            vmem((2, features, cells), low),
            vmem((features, cells), low),
            vmem((2, 2 * rows, features), full),
            vmem((2 * rows, features), full),
            vmem((rows, features), low),
            vmem((rows, features), low),
            vmem((rows // 2, features), low),
            vmem((rows // 2, features), low),
            vmem((rows // 2, features), full),
            vmem((1, length // 2), jnp.int32),
            vmem((length // 2, cells), full),
            vmem((2 * heads, 1, length), full),
            vmem((2 * heads, 1, length), full),
            vmem((2 * heads, 1, length), full),
            vmem((4, 2 * heads, cells), full),
            vmem((2 * heads, length), full),
            vmem((length // 2, DH), low),
            vmem((length // 2, DH), low),
            vmem((DH, length // 2), full),
            vmem((DH, length // 2), full),
            dma((4,)), dma((2,)), dma, dma, dma, dma((2,)), dma, dma((2,)), dma, dma((2,)),
            dma, dma((4, CHUNKS)), dma, dma, dma, dma, dma, dma((2,)),
            dma, dma((2,)), dma, dma, dma, dma, dma, dma,
            dma, dma((CHUNKS,)), dma, dma((CHUNKS,)), dma, dma((CHUNKS,)), dma((2,)),
        ],
        compiler_params=pltpu.CompilerParams(
            collective_id=0, has_side_effects=True, vmem_limit_bytes=58 << 20
        ),
    )(*arrays)


def on_device(n, queries, key_vectors, value_vectors, context, cotangent, out_weight, membership):
    features, cells = queries.shape[1], queries.shape[2]
    arrays = (queries, key_vectors, value_vectors, context, cotangent, out_weight, membership)
    if n == 8:
        return finish(paired_call(features, cells, *arrays))
    return finish(ring_call(n, *arrays))


def ring_call(n, queries, key_vectors, value_vectors, context, cotangent, out_weight, membership):
    ny = 1
    nz = n // ny
    features, cells = queries.shape[1], queries.shape[2]
    rows, length = features // n, cells * n
    heads = rows // DH
    low = jnp.bfloat16
    dma = pltpu.SemaphoreType.DMA
    anywhere = pl.BlockSpec(memory_space=pl.ANY)
    return pl.pallas_call(
        functools.partial(kernel, n, ny),
        out_shape=(
            jax.ShapeDtypeStruct(queries.shape, low),
            jax.ShapeDtypeStruct(queries.shape, low),
            jax.ShapeDtypeStruct(queries.shape, low),
            jax.ShapeDtypeStruct((rows // 2, features), jnp.float32),
        ),
        in_specs=[anywhere] * 7,
        out_specs=(anywhere,) * 4,
        scratch_shapes=[pltpu.VMEM((rows, length), low)] * 8
        + [
            pltpu.VMEM((features, length), low),
            pltpu.VMEM((rows, features), low),
            pltpu.VMEM((1, length), jnp.int32),
            pltpu.VMEM((rows, features), jnp.float32),
            pltpu.VMEM((rows // 2, features), jnp.float32),
            pltpu.VMEM((DH, length), jnp.float32),
            pltpu.VMEM((DH, length), jnp.float32),
            dma, dma, dma, dma,
            dma((4,)), dma((4, heads)),
            dma((4, nz, CHUNKS)), dma((CHUNKS, n)),
            dma((3,)), dma((3,)),
            dma, dma, dma,
        ],
        compiler_params=pltpu.CompilerParams(
            collective_id=0, has_side_effects=True, vmem_limit_bytes=56 << 20
        ),
    )(queries, key_vectors, value_vectors, context, cotangent, out_weight, membership)


def finish(parts):
    dma = pltpu.SemaphoreType.DMA
    anywhere = pl.BlockSpec(memory_space=pl.ANY)
    return pl.pallas_call(
        hand_over,
        out_shape=tuple(jax.ShapeDtypeStruct(part.shape, part.dtype) for part in parts),
        in_specs=[anywhere] * 4,
        out_specs=(anywhere,) * 4,
        scratch_shapes=[pltpu.VMEM(part.shape, part.dtype) for part in parts]
        + [dma((4,)), dma((4,))],
    )(*parts)


def solution(mesh):
    cellwise = P(("grp", "rep"), None, "seq")
    return jax.shard_map(
        functools.partial(on_device, mesh.shape["seq"]),
        mesh=mesh,
        in_specs=(cellwise,) * 5 + (P("grp", None), P(("grp", "rep"), "seq")),
        out_specs=(cellwise, cellwise, cellwise, P(("grp", "seq", "rep"), None)),
        check_vma=False,
    )
```

```python
import functools
import math

import jax
import jax.numpy as jnp
from jax import lax
from jax.experimental import pallas as pl
from jax.experimental.pallas import tpu as pltpu
from jax.sharding import PartitionSpec as P

DH = 64
MESH = pl.DeviceIdType.MESH
CHUNKS = 4
PIECES = 2


def kernel(n, ny, *refs):
    (q_ref, k_ref, v_ref, c_ref, cot_ref, w_ref, m_ref,
     dq_out, dk_out, dv_out, gw_out,
     q_buf, k_buf, v_buf, c_buf, g_buf, dq_buf, dk_buf, dv_buf,
     cot, w_buf, m_buf, gw, gw_in, k_acc, v_acc,
     w_sem, own_sem, m_send, m_recv, in_send, in_recv,
     ag_send, ag_recv, out_send, out_recv, gw_send, gw_recv, gw_sem) = refs
    me = lax.axis_index("seq")
    rep = lax.axis_index("rep")
    nz = n // ny
    z, y = me // ny, me % ny
    rows, length = q_buf.shape
    cells = length // n
    features = cot.shape[0]
    heads = rows // DH
    half = rows // 2
    piece = features // CHUNKS
    inputs = ((k_ref, k_buf), (q_ref, q_buf), (v_ref, v_buf), (c_ref, c_buf))
    outputs = ((dv_buf, dv_out), (dq_buf, dq_out), (dk_buf, dk_out))

    def cols(seq):
        return pl.ds(pl.multiple_of(seq * cells, cells), cells)

    def head_rows(h, owner=0):
        return pl.ds(pl.multiple_of(owner * rows + h * DH, DH), DH)

    barrier = pltpu.get_barrier_semaphore()
    for k in range(1, n):
        pl.semaphore_signal(barrier, inc=1, device_id={"seq": (me + k) % n}, device_id_type=MESH)
    pl.semaphore_signal(barrier, inc=1, device_id={"rep": 1 - rep}, device_id_type=MESH)

    w_copy = pltpu.make_async_copy(
        w_ref.at[pl.ds(pl.multiple_of(me * rows, rows), rows), :], w_buf, w_sem
    )
    w_copy.start()
    own_copy = pltpu.make_async_copy(cot_ref.at[0], cot.at[:, cols(me)], own_sem)
    own_copy.start()
    pltpu.make_async_copy(m_ref, m_buf.at[:, cols(me)], m_recv).start()

    pl.semaphore_wait(barrier, n)

    def ag_copy(step, part, origin, way, target):
        part_rows = pl.ds(part * piece, piece)
        landing = cot.at[part_rows, cols(origin)]
        source = cot_ref.at[0, part_rows, :] if step == 0 else landing
        return pltpu.make_async_remote_copy(
            src_ref=source,
            dst_ref=landing,
            send_sem=ag_send.at[way, step, part],
            recv_sem=ag_recv.at[part, origin],
            device_id={"seq": target},
            device_id_type=MESH,
        )

    def ag_wait(part, origin):
        landing = cot.at[pl.ds(part * piece, piece), cols(origin)]
        pltpu.make_async_copy(landing, landing, ag_recv.at[part, origin]).wait()

    def ag_step(step, arrived, send):
        for part in range(CHUNKS):
            up, down = z - step, z + step

            def act(origin, way, target):
                copy = ag_copy(step, part, origin, way, target)
                if send:
                    copy.start()
                else:
                    copy.wait_send()

            def cross(origin, way):
                if ny == 2:
                    act(origin, way, z * ny + 1 - y)

            @pl.when(up >= 0)
            def _():
                if arrived:
                    ag_wait(part, up * ny + y)

                @pl.when(z + 1 < nz)
                def _():
                    act(up * ny + y, 0, me + ny)

                cross(up * ny + y, 2)

            @pl.when(down < nz)
            def _():
                if arrived:
                    ag_wait(part, down * ny + y)

                @pl.when(z >= 1)
                def _():
                    act(down * ny + y, 1, me - ny)

                if step > 0:
                    cross(down * ny + y, 3)

    def keep_inputs(h, carry):
        for t, (ref, buf) in enumerate(inputs):
            pltpu.make_async_copy(
                ref.at[0, head_rows(h, me), :], buf.at[head_rows(h), cols(me)], in_recv.at[t, h]
            ).start()
        return carry

    def send_inputs(h, column, first):
        def to_peer(k, carry):
            peer = (z + k) % nz * ny + column
            for t, (ref, buf) in enumerate(inputs):
                pltpu.make_async_remote_copy(
                    src_ref=ref.at[0, head_rows(h, peer), :],
                    dst_ref=buf.at[head_rows(h), cols(me)],
                    send_sem=in_send.at[t],
                    recv_sem=in_recv.at[t, h],
                    device_id={"seq": peer},
                    device_id_type=MESH,
                ).start()
            return carry

        lax.fori_loop(first, nz, to_peer, 0)

    def send_members(k, carry):
        pltpu.make_async_remote_copy(
            src_ref=m_ref,
            dst_ref=m_buf.at[:, cols(me)],
            send_sem=m_send,
            recv_sem=m_recv,
            device_id={"seq": (me + k) % n},
            device_id_type=MESH,
        ).start()
        return carry

    sent = 0
    for step in range(nz):
        ag_step(step, arrived=step > 0, send=True)
        if step == 0:
            lax.fori_loop(1, n, send_members, 0)
            lax.fori_loop(0, heads, keep_inputs, 0)
        upto = -(-step * heads // nz)
        for h in range(sent, upto):
            for column, first in ((y, 1), (1 - y, 0))[:ny]:
                send_inputs(h, column, first)
        sent = upto
    for h in range(sent, heads):
        for column, first in ((y, 1), (1 - y, 0))[:ny]:
            send_inputs(h, column, first)
    if ny == 2:
        for origin_z in range(nz):
            for part in range(CHUNKS):
                ag_wait(part, origin_z * ny + 1 - y)
    own_copy.wait()
    w_copy.wait()

    block = min(256, length)

    def project(i, carry):
        at = pl.ds(pl.multiple_of(i * block, block), block)
        g_buf[:, at] = jnp.dot(
            w_buf[...], cot[:, at], preferred_element_type=jnp.float32
        ).astype(jnp.bfloat16)
        return carry

    lax.fori_loop(0, length // block, project, 0)
    pltpu.make_async_copy(m_buf, m_buf, m_recv).wait()

    scale = 1.0 / math.sqrt(DH)
    tile = 256 if length <= 2048 else 128

    def one_head(h, carry):
        mine = head_rows(h)
        for t, (_, buf) in enumerate(inputs):
            pltpu.make_async_copy(buf.at[mine], buf.at[mine], in_recv.at[t, h]).wait()
        member = m_buf[...] > 0
        keys = k_buf[mine, :]
        values = v_buf[mine, :]
        keys_scaled = keys * jnp.bfloat16(scale)
        k_acc[...] = jnp.zeros_like(k_acc)
        v_acc[...] = jnp.zeros_like(v_acc)

        def one_tile(i, inner):
            at = pl.ds(pl.multiple_of(i * tile, tile), tile)
            query = q_buf[mine, at] * jnp.bfloat16(scale)
            grad = g_buf[mine, at]
            products = grad.astype(jnp.float32) * c_buf[mine, at].astype(jnp.float32)
            delta = jnp.sum(products.T, axis=1, keepdims=True)
            first = (((0,), (0,)), ((), ()))
            scores = lax.dot_general(query, keys, first, preferred_element_type=jnp.float32)
            scores = jnp.where(member, scores, -jnp.inf)
            exps = jnp.exp(scores - jnp.max(scores, axis=1, keepdims=True))
            probs = exps * (1.0 / jnp.sum(exps, axis=1, keepdims=True))
            v_acc[...] += jnp.dot(
                grad, probs.astype(jnp.bfloat16), preferred_element_type=jnp.float32
            )
            grad_probs = lax.dot_general(grad, values, first, preferred_element_type=jnp.float32)
            grad_scores = (probs * (grad_probs - delta)).astype(jnp.bfloat16)
            dq_buf[mine, at] = lax.dot_general(
                keys_scaled, grad_scores, (((1,), (1,)), ((), ())),
                preferred_element_type=jnp.float32,
            ).astype(jnp.bfloat16)
            k_acc[...] += jnp.dot(query, grad_scores, preferred_element_type=jnp.float32)
            return inner

        lax.fori_loop(0, length // tile, one_tile, 0)
        dk_buf[mine, :] = k_acc[...].astype(jnp.bfloat16)
        dv_buf[mine, :] = v_acc[...].astype(jnp.bfloat16)
        for t, (buf, out) in enumerate(outputs):
            pltpu.make_async_copy(
                buf.at[mine, cols(me)], out.at[0, head_rows(h, me), :], out_recv.at[t]
            ).start()

        def to_peer(k, inner):
            peer = (me + k) % n
            for t, (buf, out) in enumerate(outputs):
                pltpu.make_async_remote_copy(
                    src_ref=buf.at[mine, cols(peer)],
                    dst_ref=out.at[0, head_rows(h, me), :],
                    send_sem=out_send.at[t],
                    recv_sem=out_recv.at[t],
                    device_id={"seq": peer},
                    device_id_type=MESH,
                ).start()
            return inner

        lax.fori_loop(1, n, to_peer, 0)
        return carry

    lax.fori_loop(0, heads, one_head, 0)

    width = min(256, features)

    def weight_part(i, carry):
        at = pl.ds(pl.multiple_of(i * width, width), width)
        gw[:, at] = lax.dot_general(
            c_buf[...], cot[at, :], (((1,), (1,)), ((), ())), preferred_element_type=jnp.float32
        )
        return carry

    lax.fori_loop(0, features // width, weight_part, 0)
    swap = pltpu.make_async_remote_copy(
        src_ref=gw.at[pl.ds(pl.multiple_of((1 - rep) * half, half), half), :],
        dst_ref=gw_in,
        send_sem=gw_send,
        recv_sem=gw_recv,
        device_id={"rep": 1 - rep},
        device_id_type=MESH,
    )
    swap.start()
    swap.wait()
    gw_in[...] += gw[pl.ds(pl.multiple_of(rep * half, half), half), :]
    total = pltpu.make_async_copy(gw_in, gw_out, gw_sem)
    total.start()

    for step in range(nz):
        ag_step(step, arrived=False, send=False)
    others = (n - 1) * rows
    for t, (ref, _) in enumerate(inputs):
        gone = ref.at[0, pl.ds(0, others), :]
        pltpu.make_async_copy(gone, gone, in_send.at[t]).wait()
    gone = m_buf.at[:, pl.ds(0, (n - 1) * cells)]
    pltpu.make_async_copy(gone, gone, m_send).wait()
    for t, (buf, out) in enumerate(outputs):
        gone = buf.at[:, pl.ds(0, (n - 1) * cells)]
        pltpu.make_async_copy(gone, gone, out_send.at[t]).wait()
        pltpu.make_async_copy(out, out, out_recv.at[t]).wait()
    total.wait()


def mixed(n, ny, *refs):
    (q_ref, k_ref, v_ref, c_ref, cot_ref, w_ref, m_ref,
     dq_out, dk_out, dv_out, gw_out,
     q_buf, k_buf, v_buf, c_buf, g_buf, dq_buf, dk_buf, dv_buf,
     cot, w_buf, m_buf, gw, gw_in, k_acc, v_acc,
     q_two, k_two, v_two, g_two, dq_two, dk_two, dv_two, w_two,
     exps, bias, tops, lse, lse_in, delta, k_turn, k_part, v_part, dq_in, dq_sum,
     two_send, two_recv, lse_send, lse_recv, delta_send, delta_recv, dq_send, dq_recv, sum_sem,
     w_sem, own_sem, m_send, m_recv, in_send, in_recv,
     ag_send, ag_recv, out_send, out_recv, gw_send, gw_recv, gw_sem) = refs
    me = lax.axis_index("seq")
    rep = lax.axis_index("rep")
    nz = n // ny
    z, y = me // ny, me % ny
    rows, length = q_buf.shape
    cells = length // n
    features = cot.shape[0]
    heads = rows // DH
    half = rows // 2
    piece = features // CHUNKS
    inputs = ((k_ref, k_buf), (q_ref, q_buf), (v_ref, v_buf), (c_ref, c_buf))
    outputs = ((dv_buf, dv_out), (dq_buf, dq_out), (dk_buf, dk_out))
    twin = (nz - 1 - z) * ny + y
    side = z * 2 // nz
    ours = pl.ds(pl.multiple_of(side * (length // 2), length // 2), length // 2)
    first_head = pl.ds(0, DH)
    pair_inputs = ((k_ref, k_two), (q_ref, q_two), (v_ref, v_two))

    def twin_of(seq):
        return (nz - 1 - seq // ny) * ny + seq % ny

    def near(seq):
        return seq // ny * 2 // nz == side

    def done(ref, sem):
        pltpu.make_async_copy(ref, ref, sem).wait()

    def remote(src, dst, send, recv, seq):
        pltpu.make_async_remote_copy(
            src_ref=src, dst_ref=dst, send_sem=send, recv_sem=recv,
            device_id={"seq": seq}, device_id_type=MESH,
        ).start()

    def cols(seq):
        return pl.ds(pl.multiple_of(seq * cells, cells), cells)

    def head_rows(h, owner=0):
        return pl.ds(pl.multiple_of(owner * rows + h * DH, DH), DH)

    barrier = pltpu.get_barrier_semaphore()
    for k in range(1, n):
        pl.semaphore_signal(barrier, inc=1, device_id={"seq": (me + k) % n}, device_id_type=MESH)
    pl.semaphore_signal(barrier, inc=1, device_id={"rep": 1 - rep}, device_id_type=MESH)

    w_copy = pltpu.make_async_copy(
        w_ref.at[pl.ds(pl.multiple_of(me * rows, rows), rows), :], w_buf, w_sem
    )
    w_copy.start()
    w_two_copy = pltpu.make_async_copy(w_ref.at[head_rows(0, twin), :], w_two, sum_sem)
    w_two_copy.start()
    own_copy = pltpu.make_async_copy(cot_ref.at[0], cot.at[:, cols(me)], own_sem)
    own_copy.start()
    pltpu.make_async_copy(m_ref, m_buf.at[:, cols(me)], m_recv).start()

    pl.semaphore_wait(barrier, n)

    def ag_copy(step, part, origin, way, target):
        part_rows = pl.ds(part * piece, piece)
        landing = cot.at[part_rows, cols(origin)]
        source = cot_ref.at[0, part_rows, :] if step == 0 else landing
        return pltpu.make_async_remote_copy(
            src_ref=source,
            dst_ref=landing,
            send_sem=ag_send.at[way, step, part],
            recv_sem=ag_recv.at[part, origin],
            device_id={"seq": target},
            device_id_type=MESH,
        )

    def ag_wait(part, origin):
        landing = cot.at[pl.ds(part * piece, piece), cols(origin)]
        pltpu.make_async_copy(landing, landing, ag_recv.at[part, origin]).wait()

    def ag_step(step, arrived, send):
        for part in range(CHUNKS):
            up, down = z - step, z + step

            def act(origin, way, target):
                copy = ag_copy(step, part, origin, way, target)
                if send:
                    copy.start()
                else:
                    copy.wait_send()

            def cross(origin, way):
                if ny == 2:
                    act(origin, way, z * ny + 1 - y)

            @pl.when(up >= 0)
            def _():
                if arrived:
                    ag_wait(part, up * ny + y)

                @pl.when(z + 1 < nz)
                def _():
                    act(up * ny + y, 0, me + ny)

                cross(up * ny + y, 2)

            @pl.when(down < nz)
            def _():
                if arrived:
                    ag_wait(part, down * ny + y)

                @pl.when(z >= 1)
                def _():
                    act(down * ny + y, 1, me - ny)

                if step > 0:
                    cross(down * ny + y, 3)

    def keep_inputs(h, carry):
        for t, (ref, buf) in enumerate(inputs):
            pltpu.make_async_copy(
                ref.at[0, head_rows(h, me), :], buf.at[head_rows(h), cols(me)], in_recv.at[t, h]
            ).start()
        return carry

    def keep_pair():
        for t, (ref, buf) in enumerate(pair_inputs):
            pltpu.make_async_copy(
                ref.at[0, head_rows(0, twin), :], buf.at[:, cols(me)], two_recv.at[t]
            ).start()

    def send_pair(column, first):
        def to_peer(k, carry):
            peer = (z + k) % nz * ny + column
            theirs, second = head_rows(0, peer), head_rows(0, twin_of(peer))

            def pass_on(t):
                (ref, buf), two = inputs[t], pair_inputs[t][1]
                remote(ref.at[0, theirs, :], buf.at[first_head, cols(me)],
                       in_send.at[t], in_recv.at[t, 0], peer)
                remote(ref.at[0, second, :], two.at[:, cols(me)],
                       two_send.at[t], two_recv.at[t], peer)

            pass_on(1)

            @pl.when(near(peer))
            def _():
                pass_on(0)
                pass_on(2)

            remote(c_ref.at[0, theirs, :], c_buf.at[first_head, cols(me)],
                   in_send.at[3], in_recv.at[3, 0], peer)
            return carry

        lax.fori_loop(first, nz, to_peer, 0)

    def send_inputs(h, column, first):
        def to_peer(k, carry):
            peer = (z + k) % nz * ny + column
            for t, (ref, buf) in enumerate(inputs):
                pltpu.make_async_remote_copy(
                    src_ref=ref.at[0, head_rows(h, peer), :],
                    dst_ref=buf.at[head_rows(h), cols(me)],
                    send_sem=in_send.at[t],
                    recv_sem=in_recv.at[t, h],
                    device_id={"seq": peer},
                    device_id_type=MESH,
                ).start()
            return carry

        lax.fori_loop(first, nz, to_peer, 0)

    def send_members(k, carry):
        pltpu.make_async_remote_copy(
            src_ref=m_ref,
            dst_ref=m_buf.at[:, cols(me)],
            send_sem=m_send,
            recv_sem=m_recv,
            device_id={"seq": (me + k) % n},
            device_id_type=MESH,
        ).start()
        return carry

    scale = 1.0 / math.sqrt(DH)
    tile = 256
    zero = (((0,), (0,)), ((), ()))
    last = (((1,), (1,)), ((), ()))

    def score_pair():
        done(m_buf, m_recv)
        shut = jnp.where(m_buf[:, ours] > 0, 0.0, -1e30).astype(jnp.float32)
        bias[...] = jnp.broadcast_to(shut, (bias.shape[1], length // 2)).T
        for t in (0, 1):
            arrived = inputs[t][1].at[first_head, pl.ds(0, length if t == 1 else length // 2)]
            done(arrived, in_recv.at[t, 0])
            done(pair_inputs[t][1].at[:, pl.ds(0, length if t == 1 else length // 2)], two_recv.at[t])
        for s, (keys, queries) in enumerate(((k_buf, q_buf), (k_two, q_two))):
            k_turn[...] = (keys[first_head, ours] * jnp.bfloat16(scale)).T

            def one_tile(i, inner, s=s, queries=queries):
                at = pl.ds(pl.multiple_of(i * tile, tile), tile)
                scores = jnp.dot(
                    k_turn[...], queries[first_head, at], preferred_element_type=jnp.float32
                ) + jnp.concatenate([bias[...]] * 2, axis=1)
                top = jnp.max(scores, axis=0, keepdims=True)
                grown = jnp.exp(scores - top)
                exps[s, :, at] = grown
                tops[s, :, at] = top
                lse[s, :, at] = top + jnp.log(jnp.sum(grown, axis=0, keepdims=True))
                return inner

            lax.fori_loop(0, length // tile, one_tile, 0)
        for s in range(2):
            remote(lse.at[s], lse_in.at[1 - s], lse_send, lse_recv.at[1 - s], twin)

    def share_delta():
        done(c_buf.at[first_head, :], in_recv.at[3, 0])
        products = g_buf[first_head, :].astype(jnp.float32) * c_buf[first_head, :].astype(jnp.float32)
        delta[0] = jnp.sum(products, axis=0, keepdims=True)
        remote(delta.at[0], delta.at[1], delta_send, delta_recv, twin)

    def grad_pair(s, queries, keys_of, values_of, grads_of, dq_to, dk_to, dv_to):
        done(lse_in.at[s], lse_recv.at[s])
        keys = keys_of[first_head, ours] * jnp.bfloat16(scale)
        k_turn[...] = values_of[first_head, ours].T
        k_part[...] = jnp.zeros_like(k_part)
        v_part[...] = jnp.zeros_like(v_part)

        def one_tile(i, inner):
            at = pl.ds(pl.multiple_of(i * tile, tile), tile)
            mine, theirs = lse[s, :, at], lse_in[s, :, at]
            high = jnp.maximum(mine, theirs)
            total = high + jnp.log(jnp.exp(mine - high) + jnp.exp(theirs - high))
            probs = exps[s, :, at] * jnp.exp(tops[s, :, at] - total)
            grad = grads_of[first_head, at]
            v_part[...] += lax.dot_general(
                grad, probs.astype(jnp.bfloat16), last, preferred_element_type=jnp.float32
            )
            grad_probs = jnp.dot(k_turn[...], grad, preferred_element_type=jnp.float32)
            grad_scores = (probs * (grad_probs - delta[s, :, at])).astype(jnp.bfloat16)
            dq_to[first_head, at] = jnp.dot(
                keys, grad_scores, preferred_element_type=jnp.float32
            ).astype(jnp.bfloat16)
            query = queries[first_head, at] * jnp.bfloat16(scale)
            k_part[...] += lax.dot_general(
                query, grad_scores, last, preferred_element_type=jnp.float32
            )
            return inner

        lax.fori_loop(0, length // tile, one_tile, 0)
        dk_to[first_head, ours] = k_part[...].astype(jnp.bfloat16)
        dv_to[first_head, ours] = v_part[...].astype(jnp.bfloat16)
        owner = twin if s else me
        place = pl.ds(pl.multiple_of(owner * DH, DH), DH)
        pltpu.make_async_copy(dq_to.at[first_head, cols(me)], dq_in.at[side, place, :], dq_recv).start()
        for t, buf, out in ((0, dv_to, dv_out), (2, dk_to, dk_out)):
            pltpu.make_async_copy(
                buf.at[first_head, cols(me)], out.at[0, head_rows(0, owner), :], out_recv.at[t]
            ).start()

        def to_peer(k, inner):
            peer = (me + k) % n
            remote(dq_to.at[first_head, cols(peer)], dq_in.at[side, place, :], dq_send, dq_recv, peer)

            @pl.when(near(peer))
            def _():
                for t, buf, out in ((0, dv_to, dv_out), (2, dk_to, dk_out)):
                    remote(buf.at[first_head, cols(peer)], out.at[0, head_rows(0, owner), :],
                           out_send.at[t], out_recv.at[t], peer)

            return inner

        lax.fori_loop(1, n, to_peer, 0)

    def grad_pairs():
        done(v_buf.at[first_head, pl.ds(0, length // 2)], in_recv.at[2, 0])
        done(v_two.at[:, pl.ds(0, length // 2)], two_recv.at[2])
        grad_pair(0, q_buf, k_buf, v_buf, g_buf, dq_buf, dk_buf, dv_buf)
        done(delta.at[1], delta_recv)
        grad_pair(1, q_two, k_two, v_two, g_two, dq_two, dk_two, dv_two)

    sides = ((y, 1), (1 - y, 0))[:ny]
    for step in range(nz):
        ag_step(step, arrived=step > 0, send=True)
        if step == 0:
            lax.fori_loop(1, n, send_members, 0)
            lax.fori_loop(0, heads, keep_inputs, 0)
            keep_pair()
            for column, first in sides:
                send_pair(column, first)
        elif step < heads:
            for column, first in sides:
                send_inputs(step, column, first)
        if step == nz - 2:
            score_pair()
    for h in range(nz, heads):
        for column, first in sides:
            send_inputs(h, column, first)
    own_copy.wait()
    w_copy.wait()
    w_two_copy.wait()

    block = ny * cells

    def project(i):
        at = pl.ds(pl.multiple_of(i * block, block), block)
        g_buf[:, at] = jnp.dot(
            w_buf[...], cot[:, at], preferred_element_type=jnp.float32
        ).astype(jnp.bfloat16)
        g_two[:, at] = jnp.dot(
            w_two[...], cot[:, at], preferred_element_type=jnp.float32
        ).astype(jnp.bfloat16)

    def start_head(h):
        mine = head_rows(h)
        for t, (_, buf) in enumerate(inputs):
            pltpu.make_async_copy(buf.at[mine], buf.at[mine], in_recv.at[t, h]).wait()
        k_acc[...] = jnp.zeros_like(k_acc)
        v_acc[...] = jnp.zeros_like(v_acc)

    def head_tile(h, i):
        mine = head_rows(h)
        member = m_buf[...] > 0
        keys = k_buf[mine, :]
        values = v_buf[mine, :]
        at = pl.ds(pl.multiple_of(i * tile, tile), tile)
        query = q_buf[mine, at] * jnp.bfloat16(scale)
        grad = g_buf[mine, at]
        products = grad.astype(jnp.float32) * c_buf[mine, at].astype(jnp.float32)
        sums = jnp.sum(products.T, axis=1, keepdims=True)
        scores = lax.dot_general(query, keys, zero, preferred_element_type=jnp.float32)
        scores = jnp.where(member, scores, -jnp.inf)
        grown = jnp.exp(scores - jnp.max(scores, axis=1, keepdims=True))
        probs = grown * (1.0 / jnp.sum(grown, axis=1, keepdims=True))
        v_acc[...] += jnp.dot(
            grad, probs.astype(jnp.bfloat16), preferred_element_type=jnp.float32
        )
        grad_probs = lax.dot_general(grad, values, zero, preferred_element_type=jnp.float32)
        grad_scores = (probs * (grad_probs - sums)).astype(jnp.bfloat16)
        dq_buf[mine, at] = lax.dot_general(
            keys * jnp.bfloat16(scale), grad_scores, last, preferred_element_type=jnp.float32
        ).astype(jnp.bfloat16)
        k_acc[...] += jnp.dot(query, grad_scores, preferred_element_type=jnp.float32)

    def end_head(h):
        mine = head_rows(h)
        dk_buf[mine, :] = k_acc[...].astype(jnp.bfloat16)
        dv_buf[mine, :] = v_acc[...].astype(jnp.bfloat16)
        for t, (buf, out) in enumerate(outputs):
            pltpu.make_async_copy(
                buf.at[mine, cols(me)], out.at[0, head_rows(h, me), :], out_recv.at[t]
            ).start()

        def to_peer(k, inner):
            peer = (me + k) % n
            for t, (buf, out) in enumerate(outputs):
                remote(buf.at[mine, cols(peer)], out.at[0, head_rows(h, me), :],
                       out_send.at[t], out_recv.at[t], peer)
            return inner

        lax.fori_loop(1, n, to_peer, 0)

    def one_head(h, carry):
        start_head(h)

        def one_tile(i, inner):
            head_tile(h, i)
            return inner

        lax.fori_loop(0, length // tile, one_tile, 0)
        end_head(h)
        return carry

    turn = jnp.minimum(z, nz - 1 - z)
    for k, shift in enumerate((1, 1, -2, 0)):
        place = k + turn * shift
        place = place + side * (nz - 1 - 2 * place)
        for part in range(CHUNKS):
            ag_wait(part, place * ny + 1 - y)
        project(place)
        if k == 0:
            start_head(1)
        head_tile(1, place)
    end_head(1)
    share_delta()
    one_head(2, 0)
    grad_pairs()
    one_head(3, 0)

    width = min(256, features)

    def weight_part(i, carry):
        at = pl.ds(pl.multiple_of(i * width, width), width)
        gw[:, at] = lax.dot_general(
            c_buf[...], cot[at, :], (((1,), (1,)), ((), ())), preferred_element_type=jnp.float32
        )
        return carry

    lax.fori_loop(0, features // width, weight_part, 0)
    swap = pltpu.make_async_remote_copy(
        src_ref=gw.at[pl.ds(pl.multiple_of((1 - rep) * half, half), half), :],
        dst_ref=gw_in,
        send_sem=gw_send,
        recv_sem=gw_recv,
        device_id={"rep": 1 - rep},
        device_id_type=MESH,
    )
    swap.start()
    swap.wait()
    gw_in[...] += gw[pl.ds(pl.multiple_of(rep * half, half), half), :]
    total = pltpu.make_async_copy(gw_in, gw_out, gw_sem)
    total.start()

    for step in range(nz):
        ag_step(step, arrived=False, send=False)
    whole = (n - 1) * (rows - DH)
    halves = (n // 2 - 1) * DH
    for t, (ref, _) in enumerate(inputs):
        done(ref.at[0, pl.ds(0, whole + (halves if t in (0, 2) else (n - 1) * DH)), :], in_send.at[t])
        if t < 3:
            done(ref.at[0, pl.ds(0, halves if t in (0, 2) else (n - 1) * DH), :], two_send.at[t])
    gone = m_buf.at[:, pl.ds(0, (n - 1) * cells)]
    done(gone, m_send)
    done(lse, lse_send)
    done(delta.at[0], delta_send)
    done(dq_in, dq_recv)
    dq_sum[...] = (dq_in[0].astype(jnp.float32) + dq_in[1].astype(jnp.float32)).astype(jnp.bfloat16)
    for owner in range(n):
        pltpu.make_async_copy(
            dq_sum.at[pl.ds(owner * DH, DH), :], dq_out.at[0, pl.ds(owner * rows, DH), :], sum_sem
        ).start()
    for t, (_, out) in enumerate(outputs):
        done(out.at[0, pl.ds(0, whole + (0 if t == 1 else 2 * halves)), :], out_send.at[t])
        done(out.at[0, pl.ds(0, n * (rows - (DH if t == 1 else 0))), :], out_recv.at[t])
    done(dq_buf.at[first_head, pl.ds(0, (n - 1) * cells)], dq_send)
    done(dq_buf.at[first_head, pl.ds(0, (n - 1) * cells)], dq_send)
    done(dq_sum, sum_sem)
    total.wait()


def hand_over(*refs):
    sources, targets, stages, (sem_in, sem_out) = refs[:4], refs[4:8], refs[8:12], refs[12:]
    reads, writes = [], []
    for t in (3, 0, 1, 2):
        size = stages[t].shape[-2] // PIECES
        for i in range(PIECES):
            at = (pl.ds(i * size, size),) if t == 3 else (0, pl.ds(i * size, size))
            reads.append(pltpu.make_async_copy(sources[t].at[at], stages[t].at[at], sem_in.at[t, i]))
            writes.append(pltpu.make_async_copy(stages[t].at[at], targets[t].at[at], sem_out.at[t, i]))
    for copy in reads:
        copy.start()
    for read, write in zip(reads, writes):
        read.wait()
        write.start()
    for copy in writes:
        copy.wait()


def mixed_call(n, *arrays):
    ny, nz = 2, n // 2
    features, cells = arrays[0].shape[1], arrays[0].shape[2]
    rows, length = features // n, cells * n
    heads = rows // DH
    low, full = jnp.bfloat16, jnp.float32
    dma = pltpu.SemaphoreType.DMA
    anywhere = pl.BlockSpec(memory_space=pl.ANY)
    vmem = pltpu.VMEM
    part = jax.ShapeDtypeStruct(arrays[0].shape, low)
    return pl.pallas_call(
        functools.partial(mixed, n, ny),
        out_shape=(part, part, part, jax.ShapeDtypeStruct((rows // 2, features), full)),
        in_specs=[anywhere] * 7,
        out_specs=(anywhere,) * 4,
        scratch_shapes=[vmem((rows, length), low)] * 8
        + [
            vmem((features, length), low),
            vmem((rows, features), low),
            vmem((1, length), jnp.int32),
            vmem((rows, features), full),
            vmem((rows // 2, features), full),
            vmem((DH, length), full),
            vmem((DH, length), full),
        ]
        + [vmem((DH, length), low)] * 7
        + [
            vmem((DH, features), low),
            vmem((2, length // 2, length), full),
            vmem((length // 2, 128), full),
            vmem((2, 1, length), full),
            vmem((2, 1, length), full),
            vmem((2, 1, length), full),
            vmem((2, 1, length), full),
            vmem((length // 2, DH), low),
            vmem((DH, length // 2), full),
            vmem((DH, length // 2), full),
            vmem((2, n * DH, cells), low),
            vmem((n * DH, cells), low),
            dma((3,)), dma((3,)), dma, dma((2,)), dma, dma, dma, dma, dma,
            dma, dma, dma, dma,
            dma((4,)), dma((4, heads)),
            dma((4, nz, CHUNKS)), dma((CHUNKS, n)),
            dma((3,)), dma((3,)),
            dma, dma, dma,
        ],
        compiler_params=pltpu.CompilerParams(
            collective_id=0, has_side_effects=True, vmem_limit_bytes=56 << 20
        ),
    )(*arrays)


def on_device(n, queries, key_vectors, value_vectors, context, cotangent, out_weight, membership):
    arrays = (queries, key_vectors, value_vectors, context, cotangent, out_weight, membership)
    if n == 8:
        return finish(mixed_call(n, *arrays))
    return finish(ring_call(n, *arrays))


def ring_call(n, queries, key_vectors, value_vectors, context, cotangent, out_weight, membership):
    ny = 1
    nz = n // ny
    features, cells = queries.shape[1], queries.shape[2]
    rows, length = features // n, cells * n
    heads = rows // DH
    low = jnp.bfloat16
    dma = pltpu.SemaphoreType.DMA
    anywhere = pl.BlockSpec(memory_space=pl.ANY)
    return pl.pallas_call(
        functools.partial(kernel, n, ny),
        out_shape=(
            jax.ShapeDtypeStruct(queries.shape, low),
            jax.ShapeDtypeStruct(queries.shape, low),
            jax.ShapeDtypeStruct(queries.shape, low),
            jax.ShapeDtypeStruct((rows // 2, features), jnp.float32),
        ),
        in_specs=[anywhere] * 7,
        out_specs=(anywhere,) * 4,
        scratch_shapes=[pltpu.VMEM((rows, length), low)] * 8
        + [
            pltpu.VMEM((features, length), low),
            pltpu.VMEM((rows, features), low),
            pltpu.VMEM((1, length), jnp.int32),
            pltpu.VMEM((rows, features), jnp.float32),
            pltpu.VMEM((rows // 2, features), jnp.float32),
            pltpu.VMEM((DH, length), jnp.float32),
            pltpu.VMEM((DH, length), jnp.float32),
            dma, dma, dma, dma,
            dma((4,)), dma((4, heads)),
            dma((4, nz, CHUNKS)), dma((CHUNKS, n)),
            dma((3,)), dma((3,)),
            dma, dma, dma,
        ],
        compiler_params=pltpu.CompilerParams(
            collective_id=0, has_side_effects=True, vmem_limit_bytes=56 << 20
        ),
    )(queries, key_vectors, value_vectors, context, cotangent, out_weight, membership)


def finish(parts):
    dma = pltpu.SemaphoreType.DMA
    anywhere = pl.BlockSpec(memory_space=pl.ANY)
    return pl.pallas_call(
        hand_over,
        out_shape=tuple(jax.ShapeDtypeStruct(part.shape, part.dtype) for part in parts),
        in_specs=[anywhere] * 4,
        out_specs=(anywhere,) * 4,
        scratch_shapes=[pltpu.VMEM(part.shape, part.dtype) for part in parts]
        + [dma((4, PIECES)), dma((4, PIECES))],
    )(*parts)


def solution(mesh):
    cellwise = P(("grp", "rep"), None, "seq")
    return jax.shard_map(
        functools.partial(on_device, mesh.shape["seq"]),
        mesh=mesh,
        in_specs=(cellwise,) * 5 + (P("grp", None), P(("grp", "rep"), "seq")),
        out_specs=(cellwise, cellwise, cellwise, P(("grp", "seq", "rep"), None)),
        check_vma=False,
    )
```

```python
import functools
import math

import jax
import jax.numpy as jnp
from jax import lax
from jax.experimental import pallas as pl
from jax.experimental.pallas import tpu as pltpu
from jax.sharding import PartitionSpec as P

DH = 64
MESH = pl.DeviceIdType.MESH
CHUNKS = 4
PIECES = 2


def kernel(n, ny, *refs):
    (q_ref, k_ref, v_ref, c_ref, cot_ref, w_ref, m_ref,
     dq_out, dk_out, dv_out, gw_out,
     q_buf, k_buf, v_buf, c_buf, g_buf, dq_buf, dk_buf, dv_buf,
     cot, w_buf, m_buf, gw, gw_in, k_acc, v_acc,
     w_sem, own_sem, m_send, m_recv, in_send, in_recv,
     ag_send, ag_recv, out_send, out_recv, gw_send, gw_recv, gw_sem) = refs
    me = lax.axis_index("seq")
    rep = lax.axis_index("rep")
    nz = n // ny
    z, y = me // ny, me % ny
    rows, length = q_buf.shape
    cells = length // n
    features = cot.shape[0]
    heads = rows // DH
    half = rows // 2
    piece = features // CHUNKS
    inputs = ((k_ref, k_buf), (q_ref, q_buf), (v_ref, v_buf), (c_ref, c_buf))
    outputs = ((dv_buf, dv_out), (dq_buf, dq_out), (dk_buf, dk_out))

    def cols(seq):
        return pl.ds(pl.multiple_of(seq * cells, cells), cells)

    def head_rows(h, owner=0):
        return pl.ds(pl.multiple_of(owner * rows + h * DH, DH), DH)

    barrier = pltpu.get_barrier_semaphore()
    for k in range(1, n):
        pl.semaphore_signal(barrier, inc=1, device_id={"seq": (me + k) % n}, device_id_type=MESH)
    pl.semaphore_signal(barrier, inc=1, device_id={"rep": 1 - rep}, device_id_type=MESH)

    w_copy = pltpu.make_async_copy(
        w_ref.at[pl.ds(pl.multiple_of(me * rows, rows), rows), :], w_buf, w_sem
    )
    w_copy.start()
    own_copy = pltpu.make_async_copy(cot_ref.at[0], cot.at[:, cols(me)], own_sem)
    own_copy.start()
    pltpu.make_async_copy(m_ref, m_buf.at[:, cols(me)], m_recv).start()

    pl.semaphore_wait(barrier, n)

    def ag_copy(step, part, origin, way, target):
        part_rows = pl.ds(part * piece, piece)
        landing = cot.at[part_rows, cols(origin)]
        source = cot_ref.at[0, part_rows, :] if step == 0 else landing
        return pltpu.make_async_remote_copy(
            src_ref=source,
            dst_ref=landing,
            send_sem=ag_send.at[way, step, part],
            recv_sem=ag_recv.at[part, origin],
            device_id={"seq": target},
            device_id_type=MESH,
        )

    def ag_wait(part, origin):
        landing = cot.at[pl.ds(part * piece, piece), cols(origin)]
        pltpu.make_async_copy(landing, landing, ag_recv.at[part, origin]).wait()

    def ag_step(step, arrived, send):
        for part in range(CHUNKS):
            up, down = z - step, z + step

            def act(origin, way, target):
                copy = ag_copy(step, part, origin, way, target)
                if send:
                    copy.start()
                else:
                    copy.wait_send()

            def cross(origin, way):
                if ny == 2:
                    act(origin, way, z * ny + 1 - y)

            @pl.when(up >= 0)
            def _():
                if arrived:
                    ag_wait(part, up * ny + y)

                @pl.when(z + 1 < nz)
                def _():
                    act(up * ny + y, 0, me + ny)

                cross(up * ny + y, 2)

            @pl.when(down < nz)
            def _():
                if arrived:
                    ag_wait(part, down * ny + y)

                @pl.when(z >= 1)
                def _():
                    act(down * ny + y, 1, me - ny)

                if step > 0:
                    cross(down * ny + y, 3)

    def keep_inputs(h, carry):
        for t, (ref, buf) in enumerate(inputs):
            pltpu.make_async_copy(
                ref.at[0, head_rows(h, me), :], buf.at[head_rows(h), cols(me)], in_recv.at[t, h]
            ).start()
        return carry

    def send_inputs(h, column, first):
        def to_peer(k, carry):
            peer = (z + k) % nz * ny + column
            for t, (ref, buf) in enumerate(inputs):
                pltpu.make_async_remote_copy(
                    src_ref=ref.at[0, head_rows(h, peer), :],
                    dst_ref=buf.at[head_rows(h), cols(me)],
                    send_sem=in_send.at[t],
                    recv_sem=in_recv.at[t, h],
                    device_id={"seq": peer},
                    device_id_type=MESH,
                ).start()
            return carry

        lax.fori_loop(first, nz, to_peer, 0)

    def send_members(k, carry):
        pltpu.make_async_remote_copy(
            src_ref=m_ref,
            dst_ref=m_buf.at[:, cols(me)],
            send_sem=m_send,
            recv_sem=m_recv,
            device_id={"seq": (me + k) % n},
            device_id_type=MESH,
        ).start()
        return carry

    sent = 0
    for step in range(nz):
        ag_step(step, arrived=step > 0, send=True)
        if step == 0:
            lax.fori_loop(1, n, send_members, 0)
            lax.fori_loop(0, heads, keep_inputs, 0)
        upto = -(-step * heads // nz)
        for h in range(sent, upto):
            for column, first in ((y, 1), (1 - y, 0))[:ny]:
                send_inputs(h, column, first)
        sent = upto
    for h in range(sent, heads):
        for column, first in ((y, 1), (1 - y, 0))[:ny]:
            send_inputs(h, column, first)
    if ny == 2:
        for origin_z in range(nz):
            for part in range(CHUNKS):
                ag_wait(part, origin_z * ny + 1 - y)
    own_copy.wait()
    w_copy.wait()

    block = min(256, length)

    def project(i, carry):
        at = pl.ds(pl.multiple_of(i * block, block), block)
        g_buf[:, at] = jnp.dot(
            w_buf[...], cot[:, at], preferred_element_type=jnp.float32
        ).astype(jnp.bfloat16)
        return carry

    lax.fori_loop(0, length // block, project, 0)
    pltpu.make_async_copy(m_buf, m_buf, m_recv).wait()

    scale = 1.0 / math.sqrt(DH)
    tile = 256 if length <= 2048 else 128

    def one_head(h, carry):
        mine = head_rows(h)
        for t, (_, buf) in enumerate(inputs):
            pltpu.make_async_copy(buf.at[mine], buf.at[mine], in_recv.at[t, h]).wait()
        member = m_buf[...] > 0
        keys = k_buf[mine, :]
        values = v_buf[mine, :]
        keys_scaled = keys * jnp.bfloat16(scale)
        k_acc[...] = jnp.zeros_like(k_acc)
        v_acc[...] = jnp.zeros_like(v_acc)

        def one_tile(i, inner):
            at = pl.ds(pl.multiple_of(i * tile, tile), tile)
            query = q_buf[mine, at] * jnp.bfloat16(scale)
            grad = g_buf[mine, at]
            products = grad.astype(jnp.float32) * c_buf[mine, at].astype(jnp.float32)
            delta = jnp.sum(products.T, axis=1, keepdims=True)
            first = (((0,), (0,)), ((), ()))
            scores = lax.dot_general(query, keys, first, preferred_element_type=jnp.float32)
            scores = jnp.where(member, scores, -jnp.inf)
            exps = jnp.exp(scores - jnp.max(scores, axis=1, keepdims=True))
            probs = exps * (1.0 / jnp.sum(exps, axis=1, keepdims=True))
            v_acc[...] += jnp.dot(
                grad, probs.astype(jnp.bfloat16), preferred_element_type=jnp.float32
            )
            grad_probs = lax.dot_general(grad, values, first, preferred_element_type=jnp.float32)
            grad_scores = (probs * (grad_probs - delta)).astype(jnp.bfloat16)
            dq_buf[mine, at] = lax.dot_general(
                keys_scaled, grad_scores, (((1,), (1,)), ((), ())),
                preferred_element_type=jnp.float32,
            ).astype(jnp.bfloat16)
            k_acc[...] += jnp.dot(query, grad_scores, preferred_element_type=jnp.float32)
            return inner

        lax.fori_loop(0, length // tile, one_tile, 0)
        dk_buf[mine, :] = k_acc[...].astype(jnp.bfloat16)
        dv_buf[mine, :] = v_acc[...].astype(jnp.bfloat16)
        for t, (buf, out) in enumerate(outputs):
            pltpu.make_async_copy(
                buf.at[mine, cols(me)], out.at[0, head_rows(h, me), :], out_recv.at[t]
            ).start()

        def to_peer(k, inner):
            peer = (me + k) % n
            for t, (buf, out) in enumerate(outputs):
                pltpu.make_async_remote_copy(
                    src_ref=buf.at[mine, cols(peer)],
                    dst_ref=out.at[0, head_rows(h, me), :],
                    send_sem=out_send.at[t],
                    recv_sem=out_recv.at[t],
                    device_id={"seq": peer},
                    device_id_type=MESH,
                ).start()
            return inner

        lax.fori_loop(1, n, to_peer, 0)
        return carry

    lax.fori_loop(0, heads, one_head, 0)

    width = min(256, features)

    def weight_part(i, carry):
        at = pl.ds(pl.multiple_of(i * width, width), width)
        gw[:, at] = lax.dot_general(
            c_buf[...], cot[at, :], (((1,), (1,)), ((), ())), preferred_element_type=jnp.float32
        )
        return carry

    lax.fori_loop(0, features // width, weight_part, 0)
    swap = pltpu.make_async_remote_copy(
        src_ref=gw.at[pl.ds(pl.multiple_of((1 - rep) * half, half), half), :],
        dst_ref=gw_in,
        send_sem=gw_send,
        recv_sem=gw_recv,
        device_id={"rep": 1 - rep},
        device_id_type=MESH,
    )
    swap.start()
    swap.wait()
    gw_in[...] += gw[pl.ds(pl.multiple_of(rep * half, half), half), :]
    total = pltpu.make_async_copy(gw_in, gw_out, gw_sem)
    total.start()

    for step in range(nz):
        ag_step(step, arrived=False, send=False)
    others = (n - 1) * rows
    for t, (ref, _) in enumerate(inputs):
        gone = ref.at[0, pl.ds(0, others), :]
        pltpu.make_async_copy(gone, gone, in_send.at[t]).wait()
    gone = m_buf.at[:, pl.ds(0, (n - 1) * cells)]
    pltpu.make_async_copy(gone, gone, m_send).wait()
    for t, (buf, out) in enumerate(outputs):
        gone = buf.at[:, pl.ds(0, (n - 1) * cells)]
        pltpu.make_async_copy(gone, gone, out_send.at[t]).wait()
        pltpu.make_async_copy(out, out, out_recv.at[t]).wait()
    total.wait()


def mixed(n, ny, *refs):
    (q_ref, k_ref, v_ref, c_ref, cot_ref, w_ref, m_ref,
     dq_out, dk_out, dv_out, gw_out,
     q_buf, k_buf, v_buf, c_buf, g_buf, dq_buf, dk_buf, dv_buf,
     cot, w_buf, m_buf, gw, gw_in, k_acc, v_acc,
     q_two, k_two, v_two, g_two, dq_two, dk_two, dv_two, w_two,
     exps, bias, tops, lse, lse_in, delta, k_turn, k_part, v_part, dq_in, dq_sum,
     two_send, two_recv, lse_send, lse_recv, delta_send, delta_recv, dq_send, dq_recv, sum_sem,
     w_sem, own_sem, m_send, m_recv, in_send, in_recv,
     ag_send, ag_recv, out_send, out_recv, gw_send, gw_recv, gw_sem) = refs
    me = lax.axis_index("seq")
    rep = lax.axis_index("rep")
    nz = n // ny
    z, y = me // ny, me % ny
    rows, length = q_buf.shape
    cells = length // n
    features = cot.shape[0]
    heads = rows // DH
    half = rows // 2
    piece = features // CHUNKS
    inputs = ((k_ref, k_buf), (q_ref, q_buf), (v_ref, v_buf), (c_ref, c_buf))
    outputs = ((dv_buf, dv_out), (dq_buf, dq_out), (dk_buf, dk_out))
    twin = (nz - 1 - z) * ny + y
    side = z * 2 // nz
    ours = pl.ds(pl.multiple_of(side * (length // 2), length // 2), length // 2)
    first_head = pl.ds(0, DH)
    pair_inputs = ((k_ref, k_two), (q_ref, q_two), (v_ref, v_two))

    def twin_of(seq):
        return (nz - 1 - seq // ny) * ny + seq % ny

    def near(seq):
        return seq // ny * 2 // nz == side

    def done(ref, sem):
        pltpu.make_async_copy(ref, ref, sem).wait()

    def remote(src, dst, send, recv, seq):
        pltpu.make_async_remote_copy(
            src_ref=src, dst_ref=dst, send_sem=send, recv_sem=recv,
            device_id={"seq": seq}, device_id_type=MESH,
        ).start()

    def cols(seq):
        return pl.ds(pl.multiple_of(seq * cells, cells), cells)

    def head_rows(h, owner=0):
        return pl.ds(pl.multiple_of(owner * rows + h * DH, DH), DH)

    barrier = pltpu.get_barrier_semaphore()
    for k in range(1, n):
        pl.semaphore_signal(barrier, inc=1, device_id={"seq": (me + k) % n}, device_id_type=MESH)
    pl.semaphore_signal(barrier, inc=1, device_id={"rep": 1 - rep}, device_id_type=MESH)

    w_copy = pltpu.make_async_copy(
        w_ref.at[pl.ds(pl.multiple_of(me * rows, rows), rows), :], w_buf, w_sem
    )
    w_copy.start()
    w_two_copy = pltpu.make_async_copy(w_ref.at[head_rows(0, twin), :], w_two, sum_sem)
    w_two_copy.start()
    own_copy = pltpu.make_async_copy(cot_ref.at[0], cot.at[:, cols(me)], own_sem)
    own_copy.start()
    pltpu.make_async_copy(m_ref, m_buf.at[:, cols(me)], m_recv).start()

    pl.semaphore_wait(barrier, n)

    def ag_copy(step, part, origin, way, target):
        part_rows = pl.ds(part * piece, piece)
        landing = cot.at[part_rows, cols(origin)]
        source = cot_ref.at[0, part_rows, :] if step == 0 else landing
        return pltpu.make_async_remote_copy(
            src_ref=source,
            dst_ref=landing,
            send_sem=ag_send.at[way, step, part],
            recv_sem=ag_recv.at[part, origin],
            device_id={"seq": target},
            device_id_type=MESH,
        )

    def ag_wait(part, origin):
        landing = cot.at[pl.ds(part * piece, piece), cols(origin)]
        pltpu.make_async_copy(landing, landing, ag_recv.at[part, origin]).wait()

    def ag_step(step, arrived, send):
        for part in range(CHUNKS):
            up, down = z - step, z + step

            def act(origin, way, target):
                copy = ag_copy(step, part, origin, way, target)
                if send:
                    copy.start()
                else:
                    copy.wait_send()

            def cross(origin, way):
                if ny == 2:
                    act(origin, way, z * ny + 1 - y)

            @pl.when(up >= 0)
            def _():
                if arrived:
                    ag_wait(part, up * ny + y)

                @pl.when(z + 1 < nz)
                def _():
                    act(up * ny + y, 0, me + ny)

                cross(up * ny + y, 2)

            @pl.when(down < nz)
            def _():
                if arrived:
                    ag_wait(part, down * ny + y)

                @pl.when(z >= 1)
                def _():
                    act(down * ny + y, 1, me - ny)

                if step > 0:
                    cross(down * ny + y, 3)

    def keep_inputs(h, carry):
        for t, (ref, buf) in enumerate(inputs):
            pltpu.make_async_copy(
                ref.at[0, head_rows(h, me), :], buf.at[head_rows(h), cols(me)], in_recv.at[t, h]
            ).start()
        return carry

    def keep_pair():
        for t, (ref, buf) in enumerate(pair_inputs):
            pltpu.make_async_copy(
                ref.at[0, head_rows(0, twin), :], buf.at[:, cols(me)], two_recv.at[t]
            ).start()

    def send_pair(column, first):
        def to_peer(k, carry):
            peer = (z + k) % nz * ny + column
            theirs, second = head_rows(0, peer), head_rows(0, twin_of(peer))

            def pass_on(t):
                (ref, buf), two = inputs[t], pair_inputs[t][1]
                remote(ref.at[0, theirs, :], buf.at[first_head, cols(me)],
                       in_send.at[t], in_recv.at[t, 0], peer)
                remote(ref.at[0, second, :], two.at[:, cols(me)],
                       two_send.at[t], two_recv.at[t], peer)

            pass_on(1)

            @pl.when(near(peer))
            def _():
                pass_on(0)
                pass_on(2)

            remote(c_ref.at[0, theirs, :], c_buf.at[first_head, cols(me)],
                   in_send.at[3], in_recv.at[3, 0], peer)
            return carry

        lax.fori_loop(first, nz, to_peer, 0)

    def send_inputs(h, column, first):
        def to_peer(k, carry):
            peer = (z + k) % nz * ny + column
            for t, (ref, buf) in enumerate(inputs):
                pltpu.make_async_remote_copy(
                    src_ref=ref.at[0, head_rows(h, peer), :],
                    dst_ref=buf.at[head_rows(h), cols(me)],
                    send_sem=in_send.at[t],
                    recv_sem=in_recv.at[t, h],
                    device_id={"seq": peer},
                    device_id_type=MESH,
                ).start()
            return carry

        lax.fori_loop(first, nz, to_peer, 0)

    def send_members(k, carry):
        pltpu.make_async_remote_copy(
            src_ref=m_ref,
            dst_ref=m_buf.at[:, cols(me)],
            send_sem=m_send,
            recv_sem=m_recv,
            device_id={"seq": (me + k) % n},
            device_id_type=MESH,
        ).start()
        return carry

    scale = 1.0 / math.sqrt(DH)
    tile = 256
    zero = (((0,), (0,)), ((), ()))
    last = (((1,), (1,)), ((), ()))

    def score_pair():
        done(m_buf, m_recv)
        shut = jnp.where(m_buf[:, ours] > 0, 0.0, -1e30).astype(jnp.float32)
        bias[...] = jnp.broadcast_to(shut, (bias.shape[1], length // 2)).T
        for t in (0, 1):
            arrived = inputs[t][1].at[first_head, pl.ds(0, length if t == 1 else length // 2)]
            done(arrived, in_recv.at[t, 0])
            done(pair_inputs[t][1].at[:, pl.ds(0, length if t == 1 else length // 2)], two_recv.at[t])
        for s, (keys, queries) in enumerate(((k_buf, q_buf), (k_two, q_two))):
            k_turn[...] = (keys[first_head, ours] * jnp.bfloat16(scale)).T

            def one_tile(i, inner, s=s, queries=queries):
                at = pl.ds(pl.multiple_of(i * tile, tile), tile)
                scores = jnp.dot(
                    k_turn[...], queries[first_head, at], preferred_element_type=jnp.float32
                ) + jnp.concatenate([bias[...]] * 2, axis=1)
                top = jnp.max(scores, axis=0, keepdims=True)
                grown = jnp.exp(scores - top)
                exps[s, :, at] = grown
                tops[s, :, at] = top
                lse[s, :, at] = top + jnp.log(jnp.sum(grown, axis=0, keepdims=True))
                return inner

            lax.fori_loop(0, length // tile, one_tile, 0)
        for s in range(2):
            remote(lse.at[s], lse_in.at[1 - s], lse_send, lse_recv.at[1 - s], twin)

    def share_delta():
        done(c_buf.at[first_head, :], in_recv.at[3, 0])
        products = g_buf[first_head, :].astype(jnp.float32) * c_buf[first_head, :].astype(jnp.float32)
        delta[0] = jnp.sum(products, axis=0, keepdims=True)
        remote(delta.at[0], delta.at[1], delta_send, delta_recv, twin)

    def grad_pair(s, queries, keys_of, values_of, grads_of, dq_to, dk_to, dv_to):
        done(lse_in.at[s], lse_recv.at[s])
        keys = keys_of[first_head, ours] * jnp.bfloat16(scale)
        k_turn[...] = values_of[first_head, ours].T
        k_part[...] = jnp.zeros_like(k_part)
        v_part[...] = jnp.zeros_like(v_part)

        def one_tile(i, inner):
            at = pl.ds(pl.multiple_of(i * tile, tile), tile)
            mine, theirs = lse[s, :, at], lse_in[s, :, at]
            high = jnp.maximum(mine, theirs)
            total = high + jnp.log(jnp.exp(mine - high) + jnp.exp(theirs - high))
            probs = exps[s, :, at] * jnp.exp(tops[s, :, at] - total)
            grad = grads_of[first_head, at]
            v_part[...] += lax.dot_general(
                grad, probs.astype(jnp.bfloat16), last, preferred_element_type=jnp.float32
            )
            grad_probs = jnp.dot(k_turn[...], grad, preferred_element_type=jnp.float32)
            grad_scores = (probs * (grad_probs - delta[s, :, at])).astype(jnp.bfloat16)
            dq_to[first_head, at] = jnp.dot(
                keys, grad_scores, preferred_element_type=jnp.float32
            ).astype(jnp.bfloat16)
            query = queries[first_head, at] * jnp.bfloat16(scale)
            k_part[...] += lax.dot_general(
                query, grad_scores, last, preferred_element_type=jnp.float32
            )
            return inner

        lax.fori_loop(0, length // tile, one_tile, 0)
        dk_to[first_head, ours] = k_part[...].astype(jnp.bfloat16)
        dv_to[first_head, ours] = v_part[...].astype(jnp.bfloat16)
        owner = twin if s else me
        place = pl.ds(pl.multiple_of(owner * DH, DH), DH)
        pltpu.make_async_copy(dq_to.at[first_head, cols(me)], dq_in.at[side, place, :], dq_recv).start()
        for t, buf, out in ((0, dv_to, dv_out), (2, dk_to, dk_out)):
            pltpu.make_async_copy(
                buf.at[first_head, cols(me)], out.at[0, head_rows(0, owner), :], out_recv.at[t]
            ).start()

        def to_peer(k, inner):
            peer = (me + k) % n
            remote(dq_to.at[first_head, cols(peer)], dq_in.at[side, place, :], dq_send, dq_recv, peer)

            @pl.when(near(peer))
            def _():
                for t, buf, out in ((0, dv_to, dv_out), (2, dk_to, dk_out)):
                    remote(buf.at[first_head, cols(peer)], out.at[0, head_rows(0, owner), :],
                           out_send.at[t], out_recv.at[t], peer)

            return inner

        lax.fori_loop(1, n, to_peer, 0)

    def grad_pairs():
        done(v_buf.at[first_head, pl.ds(0, length // 2)], in_recv.at[2, 0])
        done(v_two.at[:, pl.ds(0, length // 2)], two_recv.at[2])
        grad_pair(0, q_buf, k_buf, v_buf, g_buf, dq_buf, dk_buf, dv_buf)
        done(delta.at[1], delta_recv)
        grad_pair(1, q_two, k_two, v_two, g_two, dq_two, dk_two, dv_two)

    sides = ((y, 1), (1 - y, 0))[:ny]
    for step in range(nz):
        ag_step(step, arrived=step > 0, send=True)
        if step == 0:
            lax.fori_loop(1, n, send_members, 0)
            lax.fori_loop(0, heads, keep_inputs, 0)
            keep_pair()
            for column, first in sides:
                send_pair(column, first)
        elif step < heads:
            for column, first in sides:
                send_inputs(step, column, first)
        if step == nz - 2:
            score_pair()
    for h in range(nz, heads):
        for column, first in sides:
            send_inputs(h, column, first)
    own_copy.wait()
    w_copy.wait()
    w_two_copy.wait()

    block = ny * cells

    def project(i):
        at = pl.ds(pl.multiple_of(i * block, block), block)
        g_buf[:, at] = jnp.dot(
            w_buf[...], cot[:, at], preferred_element_type=jnp.float32
        ).astype(jnp.bfloat16)
        g_two[:, at] = jnp.dot(
            w_two[...], cot[:, at], preferred_element_type=jnp.float32
        ).astype(jnp.bfloat16)

    def start_head(h):
        mine = head_rows(h)
        for t, (_, buf) in enumerate(inputs):
            pltpu.make_async_copy(buf.at[mine], buf.at[mine], in_recv.at[t, h]).wait()
        k_acc[...] = jnp.zeros_like(k_acc)
        v_acc[...] = jnp.zeros_like(v_acc)

    def head_tile(h, i):
        mine = head_rows(h)
        member = m_buf[...] > 0
        keys = k_buf[mine, :]
        values = v_buf[mine, :]
        at = pl.ds(pl.multiple_of(i * tile, tile), tile)
        query = q_buf[mine, at] * jnp.bfloat16(scale)
        grad = g_buf[mine, at]
        products = grad.astype(jnp.float32) * c_buf[mine, at].astype(jnp.float32)
        sums = jnp.sum(products.T, axis=1, keepdims=True)
        scores = lax.dot_general(query, keys, zero, preferred_element_type=jnp.float32)
        scores = jnp.where(member, scores, -jnp.inf)
        grown = jnp.exp(scores - jnp.max(scores, axis=1, keepdims=True))
        probs = grown * (1.0 / jnp.sum(grown, axis=1, keepdims=True))
        v_acc[...] += jnp.dot(
            grad, probs.astype(jnp.bfloat16), preferred_element_type=jnp.float32
        )
        grad_probs = lax.dot_general(grad, values, zero, preferred_element_type=jnp.float32)
        grad_scores = (probs * (grad_probs - sums)).astype(jnp.bfloat16)
        dq_buf[mine, at] = lax.dot_general(
            keys * jnp.bfloat16(scale), grad_scores, last, preferred_element_type=jnp.float32
        ).astype(jnp.bfloat16)
        k_acc[...] += jnp.dot(query, grad_scores, preferred_element_type=jnp.float32)

    def send_queries(h, seq):
        mine, (buf, out) = head_rows(h), outputs[1]

        @pl.when(seq == me)
        def _():
            pltpu.make_async_copy(
                buf.at[mine, cols(me)], out.at[0, head_rows(h, me), :], out_recv.at[1]
            ).start()

        @pl.when(seq != me)
        def _():
            remote(buf.at[mine, cols(seq)], out.at[0, head_rows(h, me), :],
                   out_send.at[1], out_recv.at[1], seq)

    def end_head(h, kinds=(0, 1, 2)):
        mine = head_rows(h)
        dk_buf[mine, :] = k_acc[...].astype(jnp.bfloat16)
        dv_buf[mine, :] = v_acc[...].astype(jnp.bfloat16)
        for t in kinds:
            buf, out = outputs[t]
            pltpu.make_async_copy(
                buf.at[mine, cols(me)], out.at[0, head_rows(h, me), :], out_recv.at[t]
            ).start()

        def to_peer(k, inner):
            peer = (me + k) % n
            for t in kinds:
                buf, out = outputs[t]
                remote(buf.at[mine, cols(peer)], out.at[0, head_rows(h, me), :],
                       out_send.at[t], out_recv.at[t], peer)
            return inner

        lax.fori_loop(1, n, to_peer, 0)

    def one_head(h, carry):
        start_head(h)

        def one_tile(i, inner):
            head_tile(h, i)
            return inner

        lax.fori_loop(0, length // tile, one_tile, 0)
        end_head(h)
        return carry

    turn = jnp.minimum(z, nz - 1 - z)
    for k, shift in enumerate((1, 1, -2, 0)):
        place = k + turn * shift
        place = place + side * (nz - 1 - 2 * place)
        for part in range(CHUNKS):
            ag_wait(part, place * ny + 1 - y)
        project(place)
        if k == 0:
            start_head(1)
        head_tile(1, place)
        for column in (y, 1 - y):
            send_queries(1, place * ny + column)
    end_head(1, (0, 2))
    share_delta()
    one_head(2, 0)
    grad_pairs()
    one_head(3, 0)

    width = min(256, features)

    def weight_part(i, carry):
        at = pl.ds(pl.multiple_of(i * width, width), width)
        gw[:, at] = lax.dot_general(
            c_buf[...], cot[at, :], (((1,), (1,)), ((), ())), preferred_element_type=jnp.float32
        )
        return carry

    lax.fori_loop(0, features // width, weight_part, 0)
    swap = pltpu.make_async_remote_copy(
        src_ref=gw.at[pl.ds(pl.multiple_of((1 - rep) * half, half), half), :],
        dst_ref=gw_in,
        send_sem=gw_send,
        recv_sem=gw_recv,
        device_id={"rep": 1 - rep},
        device_id_type=MESH,
    )
    swap.start()
    swap.wait()
    gw_in[...] += gw[pl.ds(pl.multiple_of(rep * half, half), half), :]
    total = pltpu.make_async_copy(gw_in, gw_out, gw_sem)
    total.start()

    for step in range(nz):
        ag_step(step, arrived=False, send=False)
    whole = (n - 1) * (rows - DH)
    halves = (n // 2 - 1) * DH
    for t, (ref, _) in enumerate(inputs):
        done(ref.at[0, pl.ds(0, whole + (halves if t in (0, 2) else (n - 1) * DH)), :], in_send.at[t])
        if t < 3:
            done(ref.at[0, pl.ds(0, halves if t in (0, 2) else (n - 1) * DH), :], two_send.at[t])
    gone = m_buf.at[:, pl.ds(0, (n - 1) * cells)]
    done(gone, m_send)
    done(lse, lse_send)
    done(delta.at[0], delta_send)
    done(dq_in, dq_recv)
    dq_sum[...] = (dq_in[0].astype(jnp.float32) + dq_in[1].astype(jnp.float32)).astype(jnp.bfloat16)
    for owner in range(n):
        pltpu.make_async_copy(
            dq_sum.at[pl.ds(owner * DH, DH), :], dq_out.at[0, pl.ds(owner * rows, DH), :], sum_sem
        ).start()
    for t, (_, out) in enumerate(outputs):
        done(out.at[0, pl.ds(0, whole + (0 if t == 1 else 2 * halves)), :], out_send.at[t])
        done(out.at[0, pl.ds(0, n * (rows - (DH if t == 1 else 0))), :], out_recv.at[t])
    done(dq_buf.at[first_head, pl.ds(0, (n - 1) * cells)], dq_send)
    done(dq_buf.at[first_head, pl.ds(0, (n - 1) * cells)], dq_send)
    done(dq_sum, sum_sem)
    total.wait()


def hand_over(*refs):
    sources, targets, stages, (sem_in, sem_out) = refs[:4], refs[4:8], refs[8:12], refs[12:]
    reads, writes = [], []
    for t in (3, 0, 1, 2):
        size = stages[t].shape[-2] // PIECES
        for i in range(PIECES):
            at = (pl.ds(i * size, size),) if t == 3 else (0, pl.ds(i * size, size))
            reads.append(pltpu.make_async_copy(sources[t].at[at], stages[t].at[at], sem_in.at[t, i]))
            writes.append(pltpu.make_async_copy(stages[t].at[at], targets[t].at[at], sem_out.at[t, i]))
    for copy in reads:
        copy.start()
    for read, write in zip(reads, writes):
        read.wait()
        write.start()
    for copy in writes:
        copy.wait()


def mixed_call(n, *arrays):
    ny, nz = 2, n // 2
    features, cells = arrays[0].shape[1], arrays[0].shape[2]
    rows, length = features // n, cells * n
    heads = rows // DH
    low, full = jnp.bfloat16, jnp.float32
    dma = pltpu.SemaphoreType.DMA
    anywhere = pl.BlockSpec(memory_space=pl.ANY)
    vmem = pltpu.VMEM
    part = jax.ShapeDtypeStruct(arrays[0].shape, low)
    return pl.pallas_call(
        functools.partial(mixed, n, ny),
        out_shape=(part, part, part, jax.ShapeDtypeStruct((rows // 2, features), full)),
        in_specs=[anywhere] * 7,
        out_specs=(anywhere,) * 4,
        scratch_shapes=[vmem((rows, length), low)] * 8
        + [
            vmem((features, length), low),
            vmem((rows, features), low),
            vmem((1, length), jnp.int32),
            vmem((rows, features), full),
            vmem((rows // 2, features), full),
            vmem((DH, length), full),
            vmem((DH, length), full),
        ]
        + [vmem((DH, length), low)] * 7
        + [
            vmem((DH, features), low),
            vmem((2, length // 2, length), full),
            vmem((length // 2, 128), full),
            vmem((2, 1, length), full),
            vmem((2, 1, length), full),
            vmem((2, 1, length), full),
            vmem((2, 1, length), full),
            vmem((length // 2, DH), low),
            vmem((DH, length // 2), full),
            vmem((DH, length // 2), full),
            vmem((2, n * DH, cells), low),
            vmem((n * DH, cells), low),
            dma((3,)), dma((3,)), dma, dma((2,)), dma, dma, dma, dma, dma,
            dma, dma, dma, dma,
            dma((4,)), dma((4, heads)),
            dma((4, nz, CHUNKS)), dma((CHUNKS, n)),
            dma((3,)), dma((3,)),
            dma, dma, dma,
        ],
        compiler_params=pltpu.CompilerParams(
            collective_id=0, has_side_effects=True, vmem_limit_bytes=56 << 20
        ),
    )(*arrays)


def on_device(n, queries, key_vectors, value_vectors, context, cotangent, out_weight, membership):
    arrays = (queries, key_vectors, value_vectors, context, cotangent, out_weight, membership)
    if n == 8:
        return finish(mixed_call(n, *arrays))
    return finish(ring_call(n, *arrays))


def ring_call(n, queries, key_vectors, value_vectors, context, cotangent, out_weight, membership):
    ny = 1
    nz = n // ny
    features, cells = queries.shape[1], queries.shape[2]
    rows, length = features // n, cells * n
    heads = rows // DH
    low = jnp.bfloat16
    dma = pltpu.SemaphoreType.DMA
    anywhere = pl.BlockSpec(memory_space=pl.ANY)
    return pl.pallas_call(
        functools.partial(kernel, n, ny),
        out_shape=(
            jax.ShapeDtypeStruct(queries.shape, low),
            jax.ShapeDtypeStruct(queries.shape, low),
            jax.ShapeDtypeStruct(queries.shape, low),
            jax.ShapeDtypeStruct((rows // 2, features), jnp.float32),
        ),
        in_specs=[anywhere] * 7,
        out_specs=(anywhere,) * 4,
        scratch_shapes=[pltpu.VMEM((rows, length), low)] * 8
        + [
            pltpu.VMEM((features, length), low),
            pltpu.VMEM((rows, features), low),
            pltpu.VMEM((1, length), jnp.int32),
            pltpu.VMEM((rows, features), jnp.float32),
            pltpu.VMEM((rows // 2, features), jnp.float32),
            pltpu.VMEM((DH, length), jnp.float32),
            pltpu.VMEM((DH, length), jnp.float32),
            dma, dma, dma, dma,
            dma((4,)), dma((4, heads)),
            dma((4, nz, CHUNKS)), dma((CHUNKS, n)),
            dma((3,)), dma((3,)),
            dma, dma, dma,
        ],
        compiler_params=pltpu.CompilerParams(
            collective_id=0, has_side_effects=True, vmem_limit_bytes=56 << 20
        ),
    )(queries, key_vectors, value_vectors, context, cotangent, out_weight, membership)


def finish(parts):
    dma = pltpu.SemaphoreType.DMA
    anywhere = pl.BlockSpec(memory_space=pl.ANY)
    return pl.pallas_call(
        hand_over,
        out_shape=tuple(jax.ShapeDtypeStruct(part.shape, part.dtype) for part in parts),
        in_specs=[anywhere] * 4,
        out_specs=(anywhere,) * 4,
        scratch_shapes=[pltpu.VMEM(part.shape, part.dtype) for part in parts]
        + [dma((4, PIECES)), dma((4, PIECES))],
    )(*parts)


def solution(mesh):
    cellwise = P(("grp", "rep"), None, "seq")
    return jax.shard_map(
        functools.partial(on_device, mesh.shape["seq"]),
        mesh=mesh,
        in_specs=(cellwise,) * 5 + (P("grp", None), P(("grp", "rep"), "seq")),
        out_specs=(cellwise, cellwise, cellwise, P(("grp", "seq", "rep"), None)),
        check_vma=False,
    )
```

```python
import functools
import math

import jax
import jax.numpy as jnp
from jax import lax
from jax.experimental import pallas as pl
from jax.experimental.pallas import tpu as pltpu
from jax.sharding import PartitionSpec as P

DH = 64
MESH = pl.DeviceIdType.MESH
CHUNKS = 4
PIECES = 2


def kernel(n, ny, *refs):
    (q_ref, k_ref, v_ref, c_ref, cot_ref, w_ref, m_ref,
     dq_out, dk_out, dv_out, gw_out,
     q_buf, k_buf, v_buf, c_buf, g_buf, dq_buf, dk_buf, dv_buf,
     cot, w_buf, m_buf, gw, gw_in, k_acc, v_acc,
     w_sem, own_sem, m_send, m_recv, in_send, in_recv,
     ag_send, ag_recv, out_send, out_recv, gw_send, gw_recv, gw_sem) = refs
    me = lax.axis_index("seq")
    rep = lax.axis_index("rep")
    nz = n // ny
    z, y = me // ny, me % ny
    rows, length = q_buf.shape
    cells = length // n
    features = cot.shape[0]
    heads = rows // DH
    half = rows // 2
    piece = features // CHUNKS
    inputs = ((k_ref, k_buf), (q_ref, q_buf), (v_ref, v_buf), (c_ref, c_buf))
    outputs = ((dv_buf, dv_out), (dq_buf, dq_out), (dk_buf, dk_out))

    def cols(seq):
        return pl.ds(pl.multiple_of(seq * cells, cells), cells)

    def head_rows(h, owner=0):
        return pl.ds(pl.multiple_of(owner * rows + h * DH, DH), DH)

    barrier = pltpu.get_barrier_semaphore()
    for k in range(1, n):
        pl.semaphore_signal(barrier, inc=1, device_id={"seq": (me + k) % n}, device_id_type=MESH)
    pl.semaphore_signal(barrier, inc=1, device_id={"rep": 1 - rep}, device_id_type=MESH)

    w_copy = pltpu.make_async_copy(
        w_ref.at[pl.ds(pl.multiple_of(me * rows, rows), rows), :], w_buf, w_sem
    )
    w_copy.start()
    own_copy = pltpu.make_async_copy(cot_ref.at[0], cot.at[:, cols(me)], own_sem)
    own_copy.start()
    pltpu.make_async_copy(m_ref, m_buf.at[:, cols(me)], m_recv).start()

    pl.semaphore_wait(barrier, n)

    def ag_copy(step, part, origin, way, target):
        part_rows = pl.ds(part * piece, piece)
        landing = cot.at[part_rows, cols(origin)]
        source = cot_ref.at[0, part_rows, :] if step == 0 else landing
        return pltpu.make_async_remote_copy(
            src_ref=source,
            dst_ref=landing,
            send_sem=ag_send.at[way, step, part],
            recv_sem=ag_recv.at[part, origin],
            device_id={"seq": target},
            device_id_type=MESH,
        )

    def ag_wait(part, origin):
        landing = cot.at[pl.ds(part * piece, piece), cols(origin)]
        pltpu.make_async_copy(landing, landing, ag_recv.at[part, origin]).wait()

    def ag_step(step, arrived, send):
        for part in range(CHUNKS):
            up, down = z - step, z + step

            def act(origin, way, target):
                copy = ag_copy(step, part, origin, way, target)
                if send:
                    copy.start()
                else:
                    copy.wait_send()

            def cross(origin, way):
                if ny == 2:
                    act(origin, way, z * ny + 1 - y)

            @pl.when(up >= 0)
            def _():
                if arrived:
                    ag_wait(part, up * ny + y)

                @pl.when(z + 1 < nz)
                def _():
                    act(up * ny + y, 0, me + ny)

                cross(up * ny + y, 2)

            @pl.when(down < nz)
            def _():
                if arrived:
                    ag_wait(part, down * ny + y)

                @pl.when(z >= 1)
                def _():
                    act(down * ny + y, 1, me - ny)

                if step > 0:
                    cross(down * ny + y, 3)

    def keep_inputs(h, carry):
        for t, (ref, buf) in enumerate(inputs):
            pltpu.make_async_copy(
                ref.at[0, head_rows(h, me), :], buf.at[head_rows(h), cols(me)], in_recv.at[t, h]
            ).start()
        return carry

    def send_inputs(h, column, first):
        def to_peer(k, carry):
            peer = (z + k) % nz * ny + column
            for t, (ref, buf) in enumerate(inputs):
                pltpu.make_async_remote_copy(
                    src_ref=ref.at[0, head_rows(h, peer), :],
                    dst_ref=buf.at[head_rows(h), cols(me)],
                    send_sem=in_send.at[t],
                    recv_sem=in_recv.at[t, h],
                    device_id={"seq": peer},
                    device_id_type=MESH,
                ).start()
            return carry

        lax.fori_loop(first, nz, to_peer, 0)

    def send_members(k, carry):
        pltpu.make_async_remote_copy(
            src_ref=m_ref,
            dst_ref=m_buf.at[:, cols(me)],
            send_sem=m_send,
            recv_sem=m_recv,
            device_id={"seq": (me + k) % n},
            device_id_type=MESH,
        ).start()
        return carry

    sent = 0
    for step in range(nz):
        ag_step(step, arrived=step > 0, send=True)
        if step == 0:
            lax.fori_loop(1, n, send_members, 0)
            lax.fori_loop(0, heads, keep_inputs, 0)
        upto = -(-step * heads // nz)
        for h in range(sent, upto):
            for column, first in ((y, 1), (1 - y, 0))[:ny]:
                send_inputs(h, column, first)
        sent = upto
    for h in range(sent, heads):
        for column, first in ((y, 1), (1 - y, 0))[:ny]:
            send_inputs(h, column, first)
    if ny == 2:
        for origin_z in range(nz):
            for part in range(CHUNKS):
                ag_wait(part, origin_z * ny + 1 - y)
    own_copy.wait()
    w_copy.wait()

    block = min(256, length)

    def project(i, carry):
        at = pl.ds(pl.multiple_of(i * block, block), block)
        g_buf[:, at] = jnp.dot(
            w_buf[...], cot[:, at], preferred_element_type=jnp.float32
        ).astype(jnp.bfloat16)
        return carry

    lax.fori_loop(0, length // block, project, 0)
    pltpu.make_async_copy(m_buf, m_buf, m_recv).wait()

    scale = 1.0 / math.sqrt(DH)
    tile = 256 if length <= 2048 else 128

    def one_head(h, carry):
        mine = head_rows(h)
        for t, (_, buf) in enumerate(inputs):
            pltpu.make_async_copy(buf.at[mine], buf.at[mine], in_recv.at[t, h]).wait()
        member = m_buf[...] > 0
        keys = k_buf[mine, :]
        values = v_buf[mine, :]
        keys_scaled = keys * jnp.bfloat16(scale)
        k_acc[...] = jnp.zeros_like(k_acc)
        v_acc[...] = jnp.zeros_like(v_acc)

        def one_tile(i, inner):
            at = pl.ds(pl.multiple_of(i * tile, tile), tile)
            query = q_buf[mine, at] * jnp.bfloat16(scale)
            grad = g_buf[mine, at]
            products = grad.astype(jnp.float32) * c_buf[mine, at].astype(jnp.float32)
            delta = jnp.sum(products.T, axis=1, keepdims=True)
            first = (((0,), (0,)), ((), ()))
            scores = lax.dot_general(query, keys, first, preferred_element_type=jnp.float32)
            scores = jnp.where(member, scores, -jnp.inf)
            exps = jnp.exp(scores - jnp.max(scores, axis=1, keepdims=True))
            probs = exps * (1.0 / jnp.sum(exps, axis=1, keepdims=True))
            v_acc[...] += jnp.dot(
                grad, probs.astype(jnp.bfloat16), preferred_element_type=jnp.float32
            )
            grad_probs = lax.dot_general(grad, values, first, preferred_element_type=jnp.float32)
            grad_scores = (probs * (grad_probs - delta)).astype(jnp.bfloat16)
            dq_buf[mine, at] = lax.dot_general(
                keys_scaled, grad_scores, (((1,), (1,)), ((), ())),
                preferred_element_type=jnp.float32,
            ).astype(jnp.bfloat16)
            k_acc[...] += jnp.dot(query, grad_scores, preferred_element_type=jnp.float32)
            return inner

        lax.fori_loop(0, length // tile, one_tile, 0)
        dk_buf[mine, :] = k_acc[...].astype(jnp.bfloat16)
        dv_buf[mine, :] = v_acc[...].astype(jnp.bfloat16)
        for t, (buf, out) in enumerate(outputs):
            pltpu.make_async_copy(
                buf.at[mine, cols(me)], out.at[0, head_rows(h, me), :], out_recv.at[t]
            ).start()

        def to_peer(k, inner):
            peer = (me + k) % n
            for t, (buf, out) in enumerate(outputs):
                pltpu.make_async_remote_copy(
                    src_ref=buf.at[mine, cols(peer)],
                    dst_ref=out.at[0, head_rows(h, me), :],
                    send_sem=out_send.at[t],
                    recv_sem=out_recv.at[t],
                    device_id={"seq": peer},
                    device_id_type=MESH,
                ).start()
            return inner

        lax.fori_loop(1, n, to_peer, 0)
        return carry

    lax.fori_loop(0, heads, one_head, 0)

    width = min(256, features)

    def weight_part(i, carry):
        at = pl.ds(pl.multiple_of(i * width, width), width)
        gw[:, at] = lax.dot_general(
            c_buf[...], cot[at, :], (((1,), (1,)), ((), ())), preferred_element_type=jnp.float32
        )
        return carry

    lax.fori_loop(0, features // width, weight_part, 0)
    swap = pltpu.make_async_remote_copy(
        src_ref=gw.at[pl.ds(pl.multiple_of((1 - rep) * half, half), half), :],
        dst_ref=gw_in,
        send_sem=gw_send,
        recv_sem=gw_recv,
        device_id={"rep": 1 - rep},
        device_id_type=MESH,
    )
    swap.start()
    swap.wait()
    gw_in[...] += gw[pl.ds(pl.multiple_of(rep * half, half), half), :]
    total = pltpu.make_async_copy(gw_in, gw_out, gw_sem)
    total.start()

    for step in range(nz):
        ag_step(step, arrived=False, send=False)
    others = (n - 1) * rows
    for t, (ref, _) in enumerate(inputs):
        gone = ref.at[0, pl.ds(0, others), :]
        pltpu.make_async_copy(gone, gone, in_send.at[t]).wait()
    gone = m_buf.at[:, pl.ds(0, (n - 1) * cells)]
    pltpu.make_async_copy(gone, gone, m_send).wait()
    for t, (buf, out) in enumerate(outputs):
        gone = buf.at[:, pl.ds(0, (n - 1) * cells)]
        pltpu.make_async_copy(gone, gone, out_send.at[t]).wait()
        pltpu.make_async_copy(out, out, out_recv.at[t]).wait()
    total.wait()


def mixed(n, ny, *refs):
    (q_ref, k_ref, v_ref, c_ref, cot_ref, w_ref, m_ref,
     dq_out, dk_out, dv_out, gw_out,
     q_buf, k_buf, v_buf, c_buf, g_buf, dq_buf, dk_buf, dv_buf,
     cot, w_buf, m_buf, gw, gw_in, k_acc, v_acc,
     q_two, k_two, v_two, g_two, dq_two, dk_two, dv_two, w_two,
     exps, bias, tops, lse, lse_in, delta, k_turn, k_part, v_part, dq_in, dq_sum,
     two_send, two_recv, lse_send, lse_recv, delta_send, delta_recv, dq_send, dq_recv, sum_sem,
     w_sem, own_sem, m_send, m_recv, in_send, in_recv,
     ag_send, ag_recv, out_send, out_recv, gw_send, gw_recv, gw_sem) = refs
    me = lax.axis_index("seq")
    rep = lax.axis_index("rep")
    nz = n // ny
    z, y = me // ny, me % ny
    rows, length = q_buf.shape
    cells = length // n
    features = cot.shape[0]
    heads = rows // DH
    half = rows // 2
    piece = features // CHUNKS
    inputs = ((k_ref, k_buf), (q_ref, q_buf), (v_ref, v_buf), (c_ref, c_buf))
    outputs = ((dv_buf, dv_out), (dq_buf, dq_out), (dk_buf, dk_out))
    twin = (nz - 1 - z) * ny + y
    side = z * 2 // nz
    ours = pl.ds(pl.multiple_of(side * (length // 2), length // 2), length // 2)
    first_head = pl.ds(0, DH)
    pair_inputs = ((k_ref, k_two), (q_ref, q_two), (v_ref, v_two))

    def twin_of(seq):
        return (nz - 1 - seq // ny) * ny + seq % ny

    def near(seq):
        return seq // ny * 2 // nz == side

    def done(ref, sem):
        pltpu.make_async_copy(ref, ref, sem).wait()

    def remote(src, dst, send, recv, seq):
        pltpu.make_async_remote_copy(
            src_ref=src, dst_ref=dst, send_sem=send, recv_sem=recv,
            device_id={"seq": seq}, device_id_type=MESH,
        ).start()

    def cols(seq):
        return pl.ds(pl.multiple_of(seq * cells, cells), cells)

    def head_rows(h, owner=0):
        return pl.ds(pl.multiple_of(owner * rows + h * DH, DH), DH)

    barrier = pltpu.get_barrier_semaphore()
    for k in range(1, n):
        pl.semaphore_signal(barrier, inc=1, device_id={"seq": (me + k) % n}, device_id_type=MESH)
    pl.semaphore_signal(barrier, inc=1, device_id={"rep": 1 - rep}, device_id_type=MESH)

    w_copy = pltpu.make_async_copy(
        w_ref.at[pl.ds(pl.multiple_of(me * rows, rows), rows), :], w_buf, w_sem
    )
    w_copy.start()
    w_two_copy = pltpu.make_async_copy(w_ref.at[head_rows(0, twin), :], w_two, sum_sem)
    w_two_copy.start()
    own_copy = pltpu.make_async_copy(cot_ref.at[0], cot.at[:, cols(me)], own_sem)
    own_copy.start()
    pltpu.make_async_copy(m_ref, m_buf.at[:, cols(me)], m_recv).start()

    pl.semaphore_wait(barrier, n)

    def ag_copy(step, part, origin, way, target):
        part_rows = pl.ds(part * piece, piece)
        landing = cot.at[part_rows, cols(origin)]
        source = cot_ref.at[0, part_rows, :] if step == 0 else landing
        return pltpu.make_async_remote_copy(
            src_ref=source,
            dst_ref=landing,
            send_sem=ag_send.at[way, step, part],
            recv_sem=ag_recv.at[part, origin],
            device_id={"seq": target},
            device_id_type=MESH,
        )

    def ag_wait(part, origin):
        landing = cot.at[pl.ds(part * piece, piece), cols(origin)]
        pltpu.make_async_copy(landing, landing, ag_recv.at[part, origin]).wait()

    def ag_step(step, arrived, send):
        for part in range(CHUNKS):
            up, down = z - step, z + step

            def act(origin, way, target):
                copy = ag_copy(step, part, origin, way, target)
                if send:
                    copy.start()
                else:
                    copy.wait_send()

            def cross(origin, way):
                if ny == 2:
                    act(origin, way, z * ny + 1 - y)

            @pl.when(up >= 0)
            def _():
                if arrived:
                    ag_wait(part, up * ny + y)

                @pl.when(z + 1 < nz)
                def _():
                    act(up * ny + y, 0, me + ny)

                cross(up * ny + y, 2)

            @pl.when(down < nz)
            def _():
                if arrived:
                    ag_wait(part, down * ny + y)

                @pl.when(z >= 1)
                def _():
                    act(down * ny + y, 1, me - ny)

                if step > 0:
                    cross(down * ny + y, 3)

    def keep_inputs(h, carry):
        for t, (ref, buf) in enumerate(inputs):
            pltpu.make_async_copy(
                ref.at[0, head_rows(h, me), :], buf.at[head_rows(h), cols(me)], in_recv.at[t, h]
            ).start()
        return carry

    def keep_pair():
        for t, (ref, buf) in enumerate(pair_inputs):
            pltpu.make_async_copy(
                ref.at[0, head_rows(0, twin), :], buf.at[:, cols(me)], two_recv.at[t]
            ).start()

    def send_pair(column, first):
        def to_peer(k, carry):
            peer = (z + k) % nz * ny + column
            theirs, second = head_rows(0, peer), head_rows(0, twin_of(peer))

            def pass_on(t):
                (ref, buf), two = inputs[t], pair_inputs[t][1]
                remote(ref.at[0, theirs, :], buf.at[first_head, cols(me)],
                       in_send.at[t], in_recv.at[t, 0], peer)
                remote(ref.at[0, second, :], two.at[:, cols(me)],
                       two_send.at[t], two_recv.at[t], peer)

            pass_on(1)

            @pl.when(near(peer))
            def _():
                pass_on(0)
                pass_on(2)

            remote(c_ref.at[0, theirs, :], c_buf.at[first_head, cols(me)],
                   in_send.at[3], in_recv.at[3, 0], peer)
            return carry

        lax.fori_loop(first, nz, to_peer, 0)

    def send_inputs(h, column, first):
        def to_peer(k, carry):
            peer = (z + k) % nz * ny + column
            for t, (ref, buf) in enumerate(inputs):
                pltpu.make_async_remote_copy(
                    src_ref=ref.at[0, head_rows(h, peer), :],
                    dst_ref=buf.at[head_rows(h), cols(me)],
                    send_sem=in_send.at[t],
                    recv_sem=in_recv.at[t, h],
                    device_id={"seq": peer},
                    device_id_type=MESH,
                ).start()
            return carry

        lax.fori_loop(first, nz, to_peer, 0)

    def send_members(k, carry):
        pltpu.make_async_remote_copy(
            src_ref=m_ref,
            dst_ref=m_buf.at[:, cols(me)],
            send_sem=m_send,
            recv_sem=m_recv,
            device_id={"seq": (me + k) % n},
            device_id_type=MESH,
        ).start()
        return carry

    scale = 1.0 / math.sqrt(DH)
    tile = 256
    zero = (((0,), (0,)), ((), ()))
    last = (((1,), (1,)), ((), ()))

    def score_pair():
        done(m_buf, m_recv)
        shut = jnp.where(m_buf[:, ours] > 0, 0.0, -1e30).astype(jnp.float32)
        bias[...] = jnp.broadcast_to(shut, (bias.shape[1], length // 2)).T
        for t in (0, 1):
            arrived = inputs[t][1].at[first_head, pl.ds(0, length if t == 1 else length // 2)]
            done(arrived, in_recv.at[t, 0])
            done(pair_inputs[t][1].at[:, pl.ds(0, length if t == 1 else length // 2)], two_recv.at[t])
        for s, (keys, queries) in enumerate(((k_buf, q_buf), (k_two, q_two))):
            k_turn[...] = (keys[first_head, ours] * jnp.bfloat16(scale)).T

            def one_tile(i, inner, s=s, queries=queries):
                at = pl.ds(pl.multiple_of(i * tile, tile), tile)
                scores = jnp.dot(
                    k_turn[...], queries[first_head, at], preferred_element_type=jnp.float32
                ) + jnp.concatenate([bias[...]] * 2, axis=1)
                top = jnp.max(scores, axis=0, keepdims=True)
                grown = jnp.exp(scores - top)
                exps[s, :, at] = grown
                tops[s, :, at] = top
                lse[s, :, at] = top + jnp.log(jnp.sum(grown, axis=0, keepdims=True))
                return inner

            lax.fori_loop(0, length // tile, one_tile, 0)
        for s in range(2):
            remote(lse.at[s], lse_in.at[1 - s], lse_send, lse_recv.at[1 - s], twin)

    def share_delta():
        done(c_buf.at[first_head, :], in_recv.at[3, 0])
        products = g_buf[first_head, :].astype(jnp.float32) * c_buf[first_head, :].astype(jnp.float32)
        delta[0] = jnp.sum(products, axis=0, keepdims=True)
        remote(delta.at[0], delta.at[1], delta_send, delta_recv, twin)

    def grad_pair(s, queries, keys_of, values_of, grads_of, dq_to, dk_to, dv_to):
        done(lse_in.at[s], lse_recv.at[s])
        keys = keys_of[first_head, ours] * jnp.bfloat16(scale)
        k_turn[...] = values_of[first_head, ours].T
        k_part[...] = jnp.zeros_like(k_part)
        v_part[...] = jnp.zeros_like(v_part)

        def one_tile(i, inner):
            at = pl.ds(pl.multiple_of(i * tile, tile), tile)
            mine, theirs = lse[s, :, at], lse_in[s, :, at]
            high = jnp.maximum(mine, theirs)
            total = high + jnp.log(jnp.exp(mine - high) + jnp.exp(theirs - high))
            probs = exps[s, :, at] * jnp.exp(tops[s, :, at] - total)
            grad = grads_of[first_head, at]
            v_part[...] += lax.dot_general(
                grad, probs.astype(jnp.bfloat16), last, preferred_element_type=jnp.float32
            )
            grad_probs = jnp.dot(k_turn[...], grad, preferred_element_type=jnp.float32)
            grad_scores = (probs * (grad_probs - delta[s, :, at])).astype(jnp.bfloat16)
            dq_to[first_head, at] = jnp.dot(
                keys, grad_scores, preferred_element_type=jnp.float32
            ).astype(jnp.bfloat16)
            query = queries[first_head, at] * jnp.bfloat16(scale)
            k_part[...] += lax.dot_general(
                query, grad_scores, last, preferred_element_type=jnp.float32
            )
            return inner

        lax.fori_loop(0, length // tile, one_tile, 0)
        dk_to[first_head, ours] = k_part[...].astype(jnp.bfloat16)
        dv_to[first_head, ours] = v_part[...].astype(jnp.bfloat16)
        owner = twin if s else me
        place = pl.ds(pl.multiple_of(owner * DH, DH), DH)
        pltpu.make_async_copy(dq_to.at[first_head, cols(me)], dq_in.at[side, place, :], dq_recv).start()
        for t, buf, out in ((0, dv_to, dv_out), (2, dk_to, dk_out)):
            pltpu.make_async_copy(
                buf.at[first_head, cols(me)], out.at[0, head_rows(0, owner), :], out_recv.at[t]
            ).start()

        def to_peer(k, inner):
            peer = (me + k) % n
            remote(dq_to.at[first_head, cols(peer)], dq_in.at[side, place, :], dq_send, dq_recv, peer)

            @pl.when(near(peer))
            def _():
                for t, buf, out in ((0, dv_to, dv_out), (2, dk_to, dk_out)):
                    remote(buf.at[first_head, cols(peer)], out.at[0, head_rows(0, owner), :],
                           out_send.at[t], out_recv.at[t], peer)

            return inner

        lax.fori_loop(1, n, to_peer, 0)

    def grad_pairs():
        done(v_buf.at[first_head, pl.ds(0, length // 2)], in_recv.at[2, 0])
        done(v_two.at[:, pl.ds(0, length // 2)], two_recv.at[2])
        grad_pair(0, q_buf, k_buf, v_buf, g_buf, dq_buf, dk_buf, dv_buf)
        done(delta.at[1], delta_recv)
        grad_pair(1, q_two, k_two, v_two, g_two, dq_two, dk_two, dv_two)

    sides = ((y, 1), (1 - y, 0))[:ny]
    for step in range(nz):
        ag_step(step, arrived=step > 0, send=True)
        if step == 0:
            lax.fori_loop(1, n, send_members, 0)
            lax.fori_loop(0, heads, keep_inputs, 0)
            keep_pair()
            for column, first in sides:
                send_pair(column, first)
        elif step < heads:
            for column, first in sides:
                send_inputs(step, column, first)
        if step == nz - 2:
            score_pair()
    for h in range(nz, heads):
        for column, first in sides:
            send_inputs(h, column, first)
    own_copy.wait()
    w_copy.wait()
    w_two_copy.wait()

    block = ny * cells

    def project(i):
        at = pl.ds(pl.multiple_of(i * block, block), block)
        g_buf[:, at] = jnp.dot(
            w_buf[...], cot[:, at], preferred_element_type=jnp.float32
        ).astype(jnp.bfloat16)
        g_two[:, at] = jnp.dot(
            w_two[...], cot[:, at], preferred_element_type=jnp.float32
        ).astype(jnp.bfloat16)

    def start_head(h):
        mine = head_rows(h)
        for t, (_, buf) in enumerate(inputs):
            pltpu.make_async_copy(buf.at[mine], buf.at[mine], in_recv.at[t, h]).wait()
        k_acc[...] = jnp.zeros_like(k_acc)
        v_acc[...] = jnp.zeros_like(v_acc)

    def head_tile(h, i):
        mine = head_rows(h)
        member = m_buf[...] > 0
        keys = k_buf[mine, :]
        values = v_buf[mine, :]
        at = pl.ds(pl.multiple_of(i * tile, tile), tile)
        query = q_buf[mine, at] * jnp.bfloat16(scale)
        grad = g_buf[mine, at]
        products = grad.astype(jnp.float32) * c_buf[mine, at].astype(jnp.float32)
        sums = jnp.sum(products.T, axis=1, keepdims=True)
        scores = lax.dot_general(query, keys, zero, preferred_element_type=jnp.float32)
        scores = jnp.where(member, scores, -jnp.inf)
        grown = jnp.exp(scores - jnp.max(scores, axis=1, keepdims=True))
        probs = grown * (1.0 / jnp.sum(grown, axis=1, keepdims=True))
        v_acc[...] += jnp.dot(
            grad, probs.astype(jnp.bfloat16), preferred_element_type=jnp.float32
        )
        grad_probs = lax.dot_general(grad, values, zero, preferred_element_type=jnp.float32)
        grad_scores = (probs * (grad_probs - sums)).astype(jnp.bfloat16)
        dq_buf[mine, at] = lax.dot_general(
            keys * jnp.bfloat16(scale), grad_scores, last, preferred_element_type=jnp.float32
        ).astype(jnp.bfloat16)
        k_acc[...] += jnp.dot(query, grad_scores, preferred_element_type=jnp.float32)

    def send_queries(h, seq):
        mine, (buf, out) = head_rows(h), outputs[1]

        @pl.when(seq == me)
        def _():
            pltpu.make_async_copy(
                buf.at[mine, cols(me)], out.at[0, head_rows(h, me), :], out_recv.at[1]
            ).start()

        @pl.when(seq != me)
        def _():
            remote(buf.at[mine, cols(seq)], out.at[0, head_rows(h, me), :],
                   out_send.at[1], out_recv.at[1], seq)

    def end_head(h, kinds=(0, 1, 2)):
        mine = head_rows(h)
        dk_buf[mine, :] = k_acc[...].astype(jnp.bfloat16)
        dv_buf[mine, :] = v_acc[...].astype(jnp.bfloat16)
        for t in kinds:
            buf, out = outputs[t]
            pltpu.make_async_copy(
                buf.at[mine, cols(me)], out.at[0, head_rows(h, me), :], out_recv.at[t]
            ).start()

        def to_peer(k, inner):
            peer = (me + k) % n
            for t in kinds:
                buf, out = outputs[t]
                remote(buf.at[mine, cols(peer)], out.at[0, head_rows(h, me), :],
                       out_send.at[t], out_recv.at[t], peer)
            return inner

        lax.fori_loop(1, n, to_peer, 0)

    def one_head(h, carry):
        start_head(h)

        def one_tile(i, inner):
            head_tile(h, i)
            return inner

        lax.fori_loop(0, length // tile, one_tile, 0)
        end_head(h)
        return carry

    turn = jnp.minimum(z, nz - 1 - z)
    for k, shift in enumerate((1, 1, -2, 0)):
        place = k + turn * shift
        place = place + side * (nz - 1 - 2 * place)
        for part in range(CHUNKS):
            ag_wait(part, place * ny + 1 - y)
        project(place)
        if k == 0:
            start_head(1)
        head_tile(1, place)
        for column in (y, 1 - y):
            send_queries(1, place * ny + column)
    share_delta()
    end_head(1, (0, 2))
    one_head(2, 0)
    grad_pairs()
    one_head(3, 0)

    width = min(256, features)

    def weight_part(i, carry):
        at = pl.ds(pl.multiple_of(i * width, width), width)
        gw[:, at] = lax.dot_general(
            c_buf[...], cot[at, :], (((1,), (1,)), ((), ())), preferred_element_type=jnp.float32
        )
        return carry

    lax.fori_loop(0, features // width, weight_part, 0)
    swap = pltpu.make_async_remote_copy(
        src_ref=gw.at[pl.ds(pl.multiple_of((1 - rep) * half, half), half), :],
        dst_ref=gw_in,
        send_sem=gw_send,
        recv_sem=gw_recv,
        device_id={"rep": 1 - rep},
        device_id_type=MESH,
    )
    swap.start()
    swap.wait()
    gw_in[...] += gw[pl.ds(pl.multiple_of(rep * half, half), half), :]
    total = pltpu.make_async_copy(gw_in, gw_out, gw_sem)
    total.start()

    for step in range(nz):
        ag_step(step, arrived=False, send=False)
    whole = (n - 1) * (rows - DH)
    halves = (n // 2 - 1) * DH
    for t, (ref, _) in enumerate(inputs):
        done(ref.at[0, pl.ds(0, whole + (halves if t in (0, 2) else (n - 1) * DH)), :], in_send.at[t])
        if t < 3:
            done(ref.at[0, pl.ds(0, halves if t in (0, 2) else (n - 1) * DH), :], two_send.at[t])
    gone = m_buf.at[:, pl.ds(0, (n - 1) * cells)]
    done(gone, m_send)
    done(lse, lse_send)
    done(delta.at[0], delta_send)
    done(dq_in, dq_recv)
    dq_sum[...] = (dq_in[0].astype(jnp.float32) + dq_in[1].astype(jnp.float32)).astype(jnp.bfloat16)
    for owner in range(n):
        pltpu.make_async_copy(
            dq_sum.at[pl.ds(owner * DH, DH), :], dq_out.at[0, pl.ds(owner * rows, DH), :], sum_sem
        ).start()
    for t, (_, out) in enumerate(outputs):
        done(out.at[0, pl.ds(0, whole + (0 if t == 1 else 2 * halves)), :], out_send.at[t])
        done(out.at[0, pl.ds(0, n * (rows - (DH if t == 1 else 0))), :], out_recv.at[t])
    done(dq_buf.at[first_head, pl.ds(0, (n - 1) * cells)], dq_send)
    done(dq_buf.at[first_head, pl.ds(0, (n - 1) * cells)], dq_send)
    done(dq_sum, sum_sem)
    total.wait()


def hand_over(*refs):
    sources, targets, stages, (sem_in, sem_out) = refs[:4], refs[4:8], refs[8:12], refs[12:]
    reads, writes = [], []
    for t in (3, 0, 1, 2):
        size = stages[t].shape[-2] // PIECES
        for i in range(PIECES):
            at = (pl.ds(i * size, size),) if t == 3 else (0, pl.ds(i * size, size))
            reads.append(pltpu.make_async_copy(sources[t].at[at], stages[t].at[at], sem_in.at[t, i]))
            writes.append(pltpu.make_async_copy(stages[t].at[at], targets[t].at[at], sem_out.at[t, i]))
    for copy in reads:
        copy.start()
    for read, write in zip(reads, writes):
        read.wait()
        write.start()
    for copy in writes:
        copy.wait()


def mixed_call(n, *arrays):
    ny, nz = 2, n // 2
    features, cells = arrays[0].shape[1], arrays[0].shape[2]
    rows, length = features // n, cells * n
    heads = rows // DH
    low, full = jnp.bfloat16, jnp.float32
    dma = pltpu.SemaphoreType.DMA
    anywhere = pl.BlockSpec(memory_space=pl.ANY)
    vmem = pltpu.VMEM
    part = jax.ShapeDtypeStruct(arrays[0].shape, low)
    return pl.pallas_call(
        functools.partial(mixed, n, ny),
        out_shape=(part, part, part, jax.ShapeDtypeStruct((rows // 2, features), full)),
        in_specs=[anywhere] * 7,
        out_specs=(anywhere,) * 4,
        scratch_shapes=[vmem((rows, length), low)] * 8
        + [
            vmem((features, length), low),
            vmem((rows, features), low),
            vmem((1, length), jnp.int32),
            vmem((rows, features), full),
            vmem((rows // 2, features), full),
            vmem((DH, length), full),
            vmem((DH, length), full),
        ]
        + [vmem((DH, length), low)] * 7
        + [
            vmem((DH, features), low),
            vmem((2, length // 2, length), full),
            vmem((length // 2, 128), full),
            vmem((2, 1, length), full),
            vmem((2, 1, length), full),
            vmem((2, 1, length), full),
            vmem((2, 1, length), full),
            vmem((length // 2, DH), low),
            vmem((DH, length // 2), full),
            vmem((DH, length // 2), full),
            vmem((2, n * DH, cells), low),
            vmem((n * DH, cells), low),
            dma((3,)), dma((3,)), dma, dma((2,)), dma, dma, dma, dma, dma,
            dma, dma, dma, dma,
            dma((4,)), dma((4, heads)),
            dma((4, nz, CHUNKS)), dma((CHUNKS, n)),
            dma((3,)), dma((3,)),
            dma, dma, dma,
        ],
        compiler_params=pltpu.CompilerParams(
            collective_id=0, has_side_effects=True, vmem_limit_bytes=56 << 20
        ),
    )(*arrays)


def on_device(n, queries, key_vectors, value_vectors, context, cotangent, out_weight, membership):
    arrays = (queries, key_vectors, value_vectors, context, cotangent, out_weight, membership)
    if n == 8:
        return finish(mixed_call(n, *arrays))
    return finish(ring_call(n, *arrays))


def ring_call(n, queries, key_vectors, value_vectors, context, cotangent, out_weight, membership):
    ny = 1
    nz = n // ny
    features, cells = queries.shape[1], queries.shape[2]
    rows, length = features // n, cells * n
    heads = rows // DH
    low = jnp.bfloat16
    dma = pltpu.SemaphoreType.DMA
    anywhere = pl.BlockSpec(memory_space=pl.ANY)
    return pl.pallas_call(
        functools.partial(kernel, n, ny),
        out_shape=(
            jax.ShapeDtypeStruct(queries.shape, low),
            jax.ShapeDtypeStruct(queries.shape, low),
            jax.ShapeDtypeStruct(queries.shape, low),
            jax.ShapeDtypeStruct((rows // 2, features), jnp.float32),
        ),
        in_specs=[anywhere] * 7,
        out_specs=(anywhere,) * 4,
        scratch_shapes=[pltpu.VMEM((rows, length), low)] * 8
        + [
            pltpu.VMEM((features, length), low),
            pltpu.VMEM((rows, features), low),
            pltpu.VMEM((1, length), jnp.int32),
            pltpu.VMEM((rows, features), jnp.float32),
            pltpu.VMEM((rows // 2, features), jnp.float32),
            pltpu.VMEM((DH, length), jnp.float32),
            pltpu.VMEM((DH, length), jnp.float32),
            dma, dma, dma, dma,
            dma((4,)), dma((4, heads)),
            dma((4, nz, CHUNKS)), dma((CHUNKS, n)),
            dma((3,)), dma((3,)),
            dma, dma, dma,
        ],
        compiler_params=pltpu.CompilerParams(
            collective_id=0, has_side_effects=True, vmem_limit_bytes=56 << 20
        ),
    )(queries, key_vectors, value_vectors, context, cotangent, out_weight, membership)


def finish(parts):
    dma = pltpu.SemaphoreType.DMA
    anywhere = pl.BlockSpec(memory_space=pl.ANY)
    return pl.pallas_call(
        hand_over,
        out_shape=tuple(jax.ShapeDtypeStruct(part.shape, part.dtype) for part in parts),
        in_specs=[anywhere] * 4,
        out_specs=(anywhere,) * 4,
        scratch_shapes=[pltpu.VMEM(part.shape, part.dtype) for part in parts]
        + [dma((4, PIECES)), dma((4, PIECES))],
    )(*parts)


def solution(mesh):
    cellwise = P(("grp", "rep"), None, "seq")
    return jax.shard_map(
        functools.partial(on_device, mesh.shape["seq"]),
        mesh=mesh,
        in_specs=(cellwise,) * 5 + (P("grp", None), P(("grp", "rep"), "seq")),
        out_specs=(cellwise, cellwise, cellwise, P(("grp", "seq", "rep"), None)),
        check_vma=False,
    )
```
